512 devices in a mesh: bulk: 32 (over x, y), valve: 16 (over z, core).
Axes of the slice: x: 4, y: 8, z: 8, core: 2. Of those that a mesh axis runs over, the one named last changes fastest.
Arguments:
- right_side: float32 [5, 256, 2048], P(None, 'bulk', 'valve'), may hold values from -0.005859375 to 0.005859375
- diag_inverse: float32 [5, 5, 256, 2048], P(None, None, 'bulk', 'valve'), as said below
- lower_jacobian: float32 [5, 5, 256, 2048], P(None, None, 'bulk', 'valve')
- upper_jacobian: float32 [5, 5, 256, 2048], P(None, None, 'bulk', 'valve')
- donor_index: int32 [32, 256, 8, 128], P('bulk', 'valve'), may hold values from 0 to 1023
- donor_weight: float32 [32, 256, 8, 128], P('bulk', 'valve'), may hold values from 0 to 0.25
- point_count: int32 [32, 256], P('bulk', 'valve'), may hold values from 32 to 128, as said below
- owner_device: int32 [32, 256], P('bulk', 'valve'), may hold values from 0 to 15, as said below
Outputs:
- update: float32 [5, 256, 2048], P(None, 'bulk', 'valve')
- fringe_rows: float32 [32, 1280, 5, 128], P('bulk', 'valve')
The draws below stay inside these ranges and needn't reach their ends.
Inputs may be any that keep to these rules, and one draw needn't show every extreme that they name: `owner_device`: among the 16 blocks of one valve index at one bulk index, at most 5 name any one owner; in every draw one owner is named by exactly 5 blocks of every device. `point_count`: every device has a block with all 128 points live. `diag_inverse`: each cell's blocks are full, with nonzero entries off the diagonal.
All inputs are finite; a program needn't handle non-finite values.
Results may differ from the reference program's by a relative error of at most 0.00014.
Values sent between devices are 32-bit elements; how exact they have to be, the bound alone decides.
A program may use at most 64 MiB of HBM per device.

```python
import jax
import jax.numpy as jnp
from jax import lax

CX = 8
CY = 4
CZ = 32
DONORS = 8
POINTS = 128
ROW_BLOCKS = 16
CAPACITY = 5
MESH_SLICES = 256
NYZ = 2048
N_BULK = 32
N_VALVE = 16


def jacobian_parts(key):
    ident = jnp.eye(5, dtype=jnp.float32)[:, :, None, None]
    offdiag = 0.09 * jax.random.normal(jax.random.fold_in(key, 101), (5, 5, MESH_SLICES, NYZ), jnp.float32) * (1.0 - ident)
    scale_lo, scale_hi = (jnp.log(0.5), jnp.log(2.0))
    rate_lo, rate_hi = (jnp.log(2.3 / MESH_SLICES), jnp.log(1.0 / 30.0))
    diagonal = jnp.exp(jax.random.uniform(jax.random.fold_in(key, 102), (5, MESH_SLICES, NYZ), jnp.float32, scale_lo, scale_hi))
    damping_speeds = jnp.exp(jax.random.uniform(jax.random.fold_in(key, 103), (5, 1, NYZ), jnp.float32, rate_lo, rate_hi))
    damping_multipliers = []
    for chosen_variant in range(2):
        rough_guess = jax.random.uniform(jax.random.fold_in(key, 110 + chosen_variant), (5, MESH_SLICES, NYZ), jnp.float32, 0.5, 1.5)
        overset_pairings = jax.random.randint(jax.random.fold_in(key, 120 + chosen_variant), (1, MESH_SLICES, 1), 0, MESH_SLICES // 8) == 0
        slice_batch_cluster = jax.random.uniform(jax.random.fold_in(key, 130 + chosen_variant), (1, MESH_SLICES, 1), jnp.float32, 0.5, 0.8)
        damping_multipliers.append(jnp.exp(-damping_speeds * rough_guess) * jnp.where(overset_pairings, slice_batch_cluster, 1.0))
    return (ident, offdiag, diagonal, damping_multipliers[0], damping_multipliers[1])


def draw_diag_inverse(key, part):
    ident, offdiag, diagonal, lower_decay, upper_decay = jacobian_parts(key)
    return diagonal[:, None] * (ident + offdiag)


def draw_lower_jacobian(key, part):
    ident, offdiag, diagonal, lower_decay, upper_decay = jacobian_parts(key)
    return -(ident - offdiag) * (lower_decay / diagonal)[None, :]


def draw_upper_jacobian(key, part):
    ident, offdiag, diagonal, lower_decay, upper_decay = jacobian_parts(key)
    return -(ident - offdiag) * (upper_decay / diagonal)[None, :]


def draw_point_count(key, part):
    devices = N_BULK * N_VALVE
    counts = jax.random.randint(jax.random.fold_in(key, 201), (devices, ROW_BLOCKS), 32, POINTS + 1)
    position = jax.random.randint(jax.random.fold_in(key, 202), (devices, 1), 0, ROW_BLOCKS)
    counts = jnp.where(jnp.arange(ROW_BLOCKS)[None, :] == position, POINTS, counts)
    return counts.reshape(N_BULK, N_VALVE * ROW_BLOCKS).astype(jnp.int32)


def draw_owner_device(key, part):
    devices = N_BULK * N_VALVE
    busiest = jax.random.randint(jax.random.fold_in(key, 301), (), 0, N_VALVE)
    others_len = (N_VALVE - 1) * (CAPACITY - 1)
    turns = jnp.arange(others_len)
    other_values = (busiest + 1 + turns % (N_VALVE - 1)) % N_VALVE
    scores = jax.random.randint(jax.random.fold_in(key, 302), (devices, others_len), 0, 2 ** 20) * others_len + turns[None, :]
    order = jnp.argsort(scores, axis=1)
    picked = other_values[order[:, :ROW_BLOCKS - CAPACITY]]
    all_values = jnp.concatenate([jnp.full((devices, CAPACITY), busiest), picked], axis=1)
    scores_two = jax.random.randint(jax.random.fold_in(key, 303), (devices, ROW_BLOCKS), 0, 2 ** 20) * ROW_BLOCKS + jnp.arange(ROW_BLOCKS)[None, :]
    shuffle = jnp.argsort(scores_two, axis=1)
    result = jnp.take_along_axis(all_values, shuffle, axis=1)
    return result.reshape(N_BULK, N_VALVE * ROW_BLOCKS).astype(jnp.int32)


def plant(entries, stream_key, smallest, largest):
    longest = entries.shape.index(max(entries.shape))
    spots = []
    for shift in (0, 1):
        where = [jax.random.randint(jax.random.fold_in(stream_key, axis), (), 0, length) for axis, length in enumerate(entries.shape)]
        where[longest] = (where[longest] + shift) % entries.shape[longest]
        spots.append(tuple(where))
    return entries.at[spots[0]].set(smallest).at[spots[1]].set(largest)


def steps_of(own_key, extent, shards, least, largest):
    def one(dim, blocks):
        steps = jax.random.uniform(jax.random.fold_in(jax.random.fold_in(own_key, 6), dim), (blocks,), jnp.float32, least / len(shards), largest / len(shards))
        return jnp.repeat(jnp.exp(steps), extent[dim] // blocks).reshape((-1,) + (1,) * (len(extent) - dim - 1))

    level = one(*shards[0])
    for cut in shards[1:]:
        level = level * one(*cut)
    return level


def normal_values(own_key, dims, deviation, reach, cuts=(), kind=jnp.bfloat16):
    level = steps_of(own_key, dims, cuts, -0.22, 0.18) if cuts else 1.0
    entries = jax.random.normal(own_key, dims, jnp.float32) * deviation * level
    return jnp.minimum(jnp.maximum(entries, -reach), reach).astype(kind)


def setup_inputs(seed: int = 0) -> dict:
    splits = jax.random.split(jax.random.key(seed), 9)
    return {
        "right_side": normal_values(splits[0], (5, MESH_SLICES, NYZ), 0.001, 0.005859375, ((1, 32), (2, 16)), jnp.float32),
        "diag_inverse": draw_diag_inverse(jax.random.fold_in(splits[8], 71), 0),
        "lower_jacobian": draw_lower_jacobian(jax.random.fold_in(splits[8], 71), 0),
        "upper_jacobian": draw_upper_jacobian(jax.random.fold_in(splits[8], 71), 0),
        "donor_index": plant(jax.random.randint(splits[4], (N_BULK, N_VALVE * ROW_BLOCKS, DONORS, POINTS), 0, CX * CY * CZ), jax.random.fold_in(splits[4], 1), 0, (CX * CY * CZ) - 1).astype(jnp.int32),
        "donor_weight": jnp.clip(0.25 * jax.random.uniform(splits[5], (N_BULK, N_VALVE * ROW_BLOCKS, DONORS, POINTS), jnp.float32) ** steps_of(splits[5], (N_BULK, N_VALVE * ROW_BLOCKS, DONORS, POINTS), ((0, 32), (1, 16)), -0.2, 0.2), 0.0, 0.25),
        "point_count": draw_point_count(jax.random.fold_in(splits[8], 71), 0),
        "owner_device": draw_owner_device(jax.random.fold_in(splits[8], 71), 0),
    }


def apply_block(matrices, vectors):
    return jnp.sum(matrices * vectors[None, :, :], axis=1)


def plane_at(array, plane_index):
    return lax.dynamic_index_in_dim(array, plane_index, array.ndim - 2, keepdims=False)


def reference(right_side, diag_inverse, lower_jacobian, upper_jacobian, donor_index, donor_weight, point_count, owner_device):
    plane_width = right_side.shape[2]
    empty_state = jnp.zeros((5, plane_width), jnp.float32)

    def forward(step_index, loop_carry):
        current, written = loop_carry
        plane_index = step_index
        inverse = plane_at(diag_inverse, plane_index)
        jacobian_block = plane_at(lower_jacobian, plane_index)
        current = apply_block(inverse, plane_at(right_side, plane_index) - apply_block(jacobian_block, current))
        written = lax.dynamic_update_index_in_dim(written, current, plane_index, 1)
        return current, written

    _, starred = lax.fori_loop(0, MESH_SLICES, forward, (empty_state, jnp.zeros_like(right_side)))

    def backward(step_index, loop_carry):
        current, written = loop_carry
        plane_index = MESH_SLICES - 1 - step_index
        inverse = plane_at(diag_inverse, plane_index)
        jacobian_block = plane_at(upper_jacobian, plane_index)
        current = plane_at(starred, plane_index) - apply_block(inverse, apply_block(jacobian_block, current))
        written = lax.dynamic_update_index_in_dim(written, current, plane_index, 1)
        return current, written

    _, update = lax.fori_loop(0, MESH_SLICES, backward, (empty_state, jnp.zeros_like(right_side)))

    plane_cells = CY * CZ
    block_rows = owner_device.shape[1]
    source = (jnp.arange(block_rows) // ROW_BLOCKS).astype(jnp.int32)
    bulk_rows = jnp.arange(N_BULK).astype(jnp.int32)
    global_plane = bulk_rows[:, None, None, None] * CX + donor_index // plane_cells
    global_cell = source[None, :, None, None] * plane_cells + donor_index % plane_cells
    picked = update[:, global_plane, global_cell]
    values = jnp.sum(donor_weight[None] * picked, axis=3)
    live_mask = jnp.arange(POINTS)[None, None, :] < point_count[:, :, None]
    values = jnp.where(live_mask[None], values, jnp.float32(0.0))

    owner_grid = owner_device.reshape(N_BULK, N_VALVE, ROW_BLOCKS)
    onehot = (owner_grid[..., None] == jnp.arange(N_VALVE)).astype(jnp.int32)
    before = jnp.cumsum(onehot, axis=2) - onehot
    slot_rank = jnp.sum(onehot * before, axis=-1)
    destination = owner_grid * (N_VALVE * CAPACITY) + jnp.arange(N_VALVE)[None, :, None] * CAPACITY + slot_rank
    destination = destination.reshape(N_BULK, block_rows).astype(jnp.int32)
    fringe_rows = jnp.zeros((N_BULK, N_VALVE * N_VALVE * CAPACITY, 5, POINTS), jnp.float32)
    fringe_rows = fringe_rows.at[bulk_rows[:, None], destination].set(jnp.transpose(values, (1, 2, 0, 3)))
    return update, fringe_rows
```

```python
import functools

import jax
import jax.numpy as jnp
from jax import lax
from jax.experimental import pallas as pl
from jax.experimental.pallas import tpu as pltpu
from jax.sharding import PartitionSpec as P

NY = 8
PLANES = 8
CELLS = 128
POINTS = 128
CAPACITY = 5
ROWS = 32
MESH = pl.DeviceIdType.MESH
VMEM = pltpu.VMEM
F32 = jnp.float32


def compose(left, right):
    total = left[:, 0][:, None] * right[0][None]
    for c in range(1, 5):
        total = total + left[:, c][:, None] * right[c][None]
    return total


def apply(matrices, vectors):
    total = matrices[:, 0] * vectors[0][None]
    for c in range(1, 5):
        total = total + matrices[:, c] * vectors[c][None]
    return total


def shifted(value, amount):
    shape = value.shape
    flat = value.reshape((-1,) + shape[-2:])
    return pltpu.roll(flat, amount % shape[-2], 1).reshape(shape)


def forward_scan(matrices, offsets):
    row = lax.broadcasted_iota(jnp.int32, (8, CELLS), 0)
    for step in (1, 2, 4):
        live = row >= step
        new_offsets = offsets + apply(matrices, shifted(offsets, step))
        new_matrices = compose(matrices, shifted(matrices, step))
        offsets = jnp.where(live[None], new_offsets, offsets)
        matrices = jnp.where(live[None, None], new_matrices, matrices)
    return matrices, offsets


def backward_matrices(matrices, levels_ref):
    row = lax.broadcasted_iota(jnp.int32, (8, CELLS), 0)
    for level, step in enumerate((1, 2, 4)):
        live = row < 8 - step
        levels_ref[level] = jnp.where(live[None, None], matrices, 0.0)
        matrices = jnp.where(live[None, None], compose(matrices, shifted(matrices, -step)), matrices)
    return matrices


def backward_offsets(levels_ref, offsets):
    for level, step in enumerate((1, 2, 4)):
        offsets = offsets + apply(levels_ref[level], shifted(offsets, -step))
    return offsets


def picked_row(values, index):
    row = lax.broadcasted_iota(jnp.int32, (8, CELLS), 0)
    kept = jnp.where((row == index)[None], values, 0.0)
    for step in (1, 2, 4):
        kept = kept + shifted(kept, step)
    return kept


def sweep_kernel(
    nx,
    rhs_ref,
    diag_ref,
    lower_ref,
    upper_ref,
    update_ref,
    low_out,
    low_all,
    low_total,
    low_rows,
    up_out,
    up_all,
    up_total,
    up_rows,
    off_out,
    off_all,
    off_total,
    off_rows,
    plane_levels,
    row_levels,
    y_send,
    y_recv,
    x_send,
    x_recv,
):
    bulk = lax.axis_index("bulk")
    my_x = bulk // NY
    my_y = bulk % NY

    def y_peer(step):
        return {"bulk": my_x * NY + (my_y + step) % NY}

    def x_peer(step):
        return {"bulk": ((my_x + step) % nx) * NY + my_y}

    barrier = pltpu.get_barrier_semaphore()
    for step in range(1, NY):
        pl.semaphore_signal(barrier, inc=1, device_id=y_peer(step), device_id_type=MESH)
    for step in range(1, nx):
        pl.semaphore_signal(barrier, inc=1, device_id=x_peer(step), device_id_type=MESH)

    def place(ref, index, rows):
        return ref.at[pl.ds(pl.multiple_of(index * rows, 8), rows), :]

    def send_y(stage, source, target, rows):
        copies = []
        for step in (4, 3, 5, 2, 6, 1, 7):
            copy = pltpu.make_async_remote_copy(
                src_ref=source,
                dst_ref=place(target, my_y, rows),
                send_sem=y_send.at[stage, step - 1],
                recv_sem=y_recv.at[stage, step - 1],
                device_id=y_peer(step),
                device_id_type=MESH,
            )
            copy.start()
            copies.append(copy)
        return copies

    def send_x(stage, source, target, rows):
        copies = []
        for step in range(1, nx):
            copy = pltpu.make_async_remote_copy(
                src_ref=source,
                dst_ref=place(target, my_x, rows),
                send_sem=x_send.at[stage, step - 1],
                recv_sem=x_recv.at[stage, step - 1],
                device_id=x_peer(step),
                device_id_type=MESH,
            )
            copy.start()
            copies.append(copy)
        return copies

    def arrive(copies):
        for copy in copies:
            copy.wait_recv()

    def put(ref, first, value, row):
        for index in range(value.shape[0]):
            ref[first + index : first + index + 1, :] = value[index, row : row + 1, :]

    def gathered(ref, first, count, stride):
        return jnp.stack([ref[pl.ds(first + index, 8, stride=stride), :] for index in range(count)])

    diag = diag_ref[...]
    low_matrices, low_offsets = forward_scan(-compose(diag, lower_ref[...]), apply(diag, rhs_ref[...]))
    put(low_out, 0, low_matrices.reshape(25, PLANES, CELLS), PLANES - 1)
    put(low_out, 25, low_offsets, PLANES - 1)
    place(low_all, my_y, ROWS)[...] = low_out[...]
    pl.semaphore_wait(barrier, NY + nx - 2)
    low_y = send_y(0, low_out, low_all, ROWS)

    up_matrices = backward_matrices(-compose(diag, upper_ref[...]), plane_levels)
    put(up_out, 0, up_matrices.reshape(25, PLANES, CELLS), 0)
    place(up_all, my_y, ROWS)[...] = up_out[...]
    up_y = send_y(1, up_out, up_all, ROWS)

    arrive(low_y)
    row_matrices, row_offsets = forward_scan(
        gathered(low_all, 0, 25, ROWS).reshape(5, 5, 8, CELLS), gathered(low_all, 25, 5, ROWS)
    )
    put(low_total, 0, row_matrices.reshape(25, 8, CELLS), 7)
    put(low_total, 25, row_offsets, 7)
    low_x = send_x(0, low_total, low_rows, ROWS)

    arrive(up_y)
    row_up = backward_matrices(gathered(up_all, 0, 25, ROWS).reshape(5, 5, 8, CELLS), row_levels)
    put(up_total, 0, row_up.reshape(25, 8, CELLS), 0)
    up_x = send_x(1, up_total, up_rows, ROWS)

    place(low_rows, my_x, ROWS)[...] = low_total[...]
    place(up_rows, my_x, ROWS)[...] = up_total[...]

    def chain(rows, offsets_of, order, passes):
        state = [jnp.zeros((1, CELLS), F32) for _ in range(5)]
        for x in order:
            offsets = offsets_of(x)
            new_state = []
            for a in range(5):
                value = offsets[a]
                for b in range(5):
                    at = x * ROWS + a * 5 + b
                    value = value + rows[at : at + 1, :] * state[b]
                new_state.append(value)
            keep = passes(x)
            state = [jnp.where(keep, new, old) for new, old in zip(new_state, state)]
        return jnp.stack([jnp.broadcast_to(value, (8, CELLS)) for value in state])

    arrive(low_x)
    entering = chain(
        low_rows,
        lambda x: [low_rows[x * ROWS + 25 + a : x * ROWS + 26 + a, :] for a in range(5)],
        range(nx - 1),
        lambda x: x < my_x,
    )
    leaving = row_offsets + apply(row_matrices, entering)
    incoming = jnp.where(my_y == 0, entering, picked_row(leaving, my_y - 1))
    starred = low_offsets + apply(low_matrices, incoming)

    partial = backward_offsets(plane_levels, starred)
    put(off_out, 0, partial, 0)
    off_y = send_y(2, off_out, off_all, 8)
    place(off_all, my_y, 8)[...] = off_out[...]
    arrive(up_x)
    arrive(off_y)
    row_partial = backward_offsets(row_levels, gathered(off_all, 0, 5, 8))
    put(off_total, 0, row_partial, 0)
    off_x = send_x(2, off_total, off_rows, 8)
    place(off_rows, my_x, 8)[...] = off_total[...]
    arrive(off_x)
    entering = chain(
        up_rows,
        lambda x: [off_rows[x * 8 + a : x * 8 + a + 1, :] for a in range(5)],
        range(nx - 1, 0, -1),
        lambda x: x > my_x,
    )
    leaving = row_partial + apply(row_up, entering)
    incoming = jnp.where(my_y == NY - 1, entering, picked_row(leaving, my_y + 1))
    update_ref[...] = partial + apply(up_matrices, incoming)

    for copies in (low_y, up_y, low_x, up_x, off_y, off_x):
        for copy in copies:
            copy.wait_send()


def sweeps(nx, rhs, diag, lower, upper):
    return pl.pallas_call(
        functools.partial(sweep_kernel, nx),
        out_shape=jax.ShapeDtypeStruct((5, PLANES, CELLS), F32),
        in_specs=[pl.BlockSpec(memory_space=VMEM)] * 4,
        out_specs=pl.BlockSpec(memory_space=VMEM),
        scratch_shapes=[
            VMEM((ROWS, CELLS), F32),
            VMEM((NY * ROWS, CELLS), F32),
            VMEM((ROWS, CELLS), F32),
            VMEM((nx * ROWS, CELLS), F32),
            VMEM((ROWS, CELLS), F32),
            VMEM((NY * ROWS, CELLS), F32),
            VMEM((ROWS, CELLS), F32),
            VMEM((nx * ROWS, CELLS), F32),
            VMEM((8, CELLS), F32),
            VMEM((NY * 8, CELLS), F32),
            VMEM((8, CELLS), F32),
            VMEM((nx * 8, CELLS), F32),
            VMEM((3, 5, 5, 8, CELLS), F32),
            VMEM((3, 5, 5, 8, CELLS), F32),
            pltpu.SemaphoreType.DMA((3, NY - 1)),
            pltpu.SemaphoreType.DMA((3, NY - 1)),
            pltpu.SemaphoreType.DMA((3, max(nx - 1, 1))),
            pltpu.SemaphoreType.DMA((3, max(nx - 1, 1))),
        ],
        compiler_params=pltpu.CompilerParams(collective_id=0, has_side_effects=True),
    )(rhs, diag, lower, upper)


def fringe_kernel(
    nv,
    count_ref,
    owner_ref,
    owner_row_ref,
    update_ref,
    index_ref,
    weight_ref,
    out_ref,
    table,
    values,
    outgoing,
    arrived,
    send_sem,
    recv_sem,
):
    me = lax.axis_index("valve")
    blocks = index_ref.shape[0]
    barrier = pltpu.get_barrier_semaphore()
    for step in range(1, nv):
        pl.semaphore_signal(barrier, inc=1, device_id={"valve": (me + step) % nv}, device_id_type=MESH)

    for c in range(5):
        for plane in range(PLANES):
            table[c, plane] = jnp.broadcast_to(update_ref[c, plane : plane + 1, :], (8, CELLS))
    lane = lax.broadcasted_iota(jnp.int32, (1, POINTS), 1)

    def interpolate(block, carry):
        donors = index_ref[block]
        weights = weight_ref[block]
        cell = donors & (CELLS - 1)
        plane_of = donors >> 7
        live = lane < count_ref[0, block]
        here = [plane_of == plane for plane in range(PLANES)]
        for c in range(5):
            picked = jnp.take_along_axis(table[c, 0], cell, axis=1, mode="promise_in_bounds")
            for plane in range(1, PLANES):
                other = jnp.take_along_axis(table[c, plane], cell, axis=1, mode="promise_in_bounds")
                picked = jnp.where(here[plane], other, picked)
            total = jnp.sum(weights * picked, axis=0, keepdims=True)
            values[c, pl.ds(block, 1), :] = jnp.where(live, total, 0.0)
        return carry

    lax.fori_loop(0, blocks, interpolate, 0)

    owner = owner_row_ref[...]
    position = lax.broadcasted_iota(jnp.int32, (1, blocks), 1)
    rank = jnp.zeros((1, blocks), jnp.int32)
    for earlier in range(blocks):
        same = (owner == owner_ref[0, earlier]) & (position > earlier)
        rank = rank + jnp.where(same, 1, 0)
    target = owner * 8 + rank
    slot = lax.broadcasted_iota(jnp.int32, (nv * 8, blocks), 0)
    placement = jnp.where(slot == target, 1.0, 0.0).astype(F32)
    for c in range(5):
        rows = jnp.dot(placement, values[c], precision=lax.Precision.HIGHEST, preferred_element_type=F32)
        outgoing[:, c] = rows.reshape(nv, 8, POINTS)

    pl.semaphore_wait(barrier, nv - 1)
    copies = []
    for step in range(1, nv):
        peer = (me + step) % nv
        copy = pltpu.make_async_remote_copy(
            src_ref=outgoing.at[peer],
            dst_ref=arrived.at[me],
            send_sem=send_sem.at[step - 1],
            recv_sem=recv_sem.at[step - 1],
            device_id={"valve": peer},
            device_id_type=MESH,
        )
        copy.start()
        copies.append(copy)
    arrived[me] = outgoing[me]
    for copy in copies:
        copy.wait_recv()
    for source in range(nv):
        for c in range(5):
            out_ref[c, source * CAPACITY : (source + 1) * CAPACITY, :] = arrived[source, c, 0:CAPACITY, :]
    for copy in copies:
        copy.wait_send()


def fringe(nv, count, owner, update, index, weight):
    blocks = index.shape[0]
    smem = pl.BlockSpec(memory_space=pltpu.SMEM)
    vmem = pl.BlockSpec(memory_space=VMEM)
    return pl.pallas_call(
        functools.partial(fringe_kernel, nv),
        out_shape=jax.ShapeDtypeStruct((5, nv * CAPACITY, POINTS), F32),
        in_specs=[smem, smem, vmem, vmem, vmem, vmem],
        out_specs=vmem,
        scratch_shapes=[
            VMEM((5, PLANES, 8, CELLS), F32),
            VMEM((5, blocks, POINTS), F32),
            VMEM((nv, 5, 8, POINTS), F32),
            VMEM((nv, 5, 8, POINTS), F32),
            pltpu.SemaphoreType.DMA((nv - 1,)),
            pltpu.SemaphoreType.DMA((nv - 1,)),
        ],
        compiler_params=pltpu.CompilerParams(collective_id=1, has_side_effects=True),
    )(count, owner, owner, update, index, weight)


def solution(mesh):
    nx = mesh.shape["bulk"] // NY
    nv = mesh.shape["valve"]

    def body(rhs, diag, lower, upper, index, weight, count, owner):
        update = sweeps(nx, rhs, diag, lower, upper)
        rows = fringe(nv, count, owner, update, index[0], weight[0])
        return update, jnp.transpose(rows, (1, 0, 2))[None]

    in_specs = (
        P(None, "bulk", "valve"),
        P(None, None, "bulk", "valve"),
        P(None, None, "bulk", "valve"),
        P(None, None, "bulk", "valve"),
        P("bulk", "valve", None, None),
        P("bulk", "valve", None, None),
        P("bulk", "valve"),
        P("bulk", "valve"),
    )
    out_specs = (P(None, "bulk", "valve"), P("bulk", "valve", None, None))
    return jax.shard_map(body, mesh=mesh, in_specs=in_specs, out_specs=out_specs, check_vma=False)
```

```python
import functools

import jax
import jax.numpy as jnp
from jax import lax
from jax.experimental import pallas as pl
from jax.experimental.pallas import tpu as pltpu
from jax.sharding import PartitionSpec as P

NY = 8
PLANES = 8
CELLS = 128
POINTS = 128
CAPACITY = 5
ROWS = 32
BLOCKS = 16
MESH = pl.DeviceIdType.MESH
VMEM = pltpu.VMEM
F32 = jnp.float32


def compose(left, right):
    total = left[:, 0][:, None] * right[0][None]
    for c in range(1, 5):
        total = total + left[:, c][:, None] * right[c][None]
    return total


def apply(matrices, vectors):
    total = matrices[:, 0] * vectors[0][None]
    for c in range(1, 5):
        total = total + matrices[:, c] * vectors[c][None]
    return total


def shifted(value, amount):
    shape = value.shape
    flat = value.reshape((-1,) + shape[-2:])
    return pltpu.roll(flat, amount % shape[-2], 1).reshape(shape)


def forward_scan(matrices, offsets):
    row = lax.broadcasted_iota(jnp.int32, (8, CELLS), 0)
    for step in (1, 2, 4):
        live = row >= step
        new_offsets = offsets + apply(matrices, shifted(offsets, step))
        new_matrices = compose(matrices, shifted(matrices, step))
        offsets = jnp.where(live[None], new_offsets, offsets)
        matrices = jnp.where(live[None, None], new_matrices, matrices)
    return matrices, offsets


def backward_matrices(matrices, levels_ref):
    row = lax.broadcasted_iota(jnp.int32, (8, CELLS), 0)
    for level, step in enumerate((1, 2, 4)):
        live = row < 8 - step
        levels_ref[level] = jnp.where(live[None, None], matrices, 0.0)
        matrices = jnp.where(live[None, None], compose(matrices, shifted(matrices, -step)), matrices)
    return matrices


def backward_offsets(levels_ref, offsets):
    for level, step in enumerate((1, 2, 4)):
        offsets = offsets + apply(levels_ref[level], shifted(offsets, -step))
    return offsets


def picked_row(values, index):
    row = lax.broadcasted_iota(jnp.int32, (8, CELLS), 0)
    kept = jnp.where((row == index)[None], values, 0.0)
    for step in (1, 2, 4):
        kept = kept + shifted(kept, step)
    return kept


def whole_kernel(
    nx,
    nv,
    rhs_hbm,
    diag_hbm,
    lower_hbm,
    upper_hbm,
    index_hbm,
    weight_hbm,
    count_hbm,
    owner_hbm,
    update_ref,
    fringe_ref,
    rhs_ref,
    diag_ref,
    lower_ref,
    upper_ref,
    index_ref,
    weight_ref,
    count_ref,
    owner_ref,
    low_out,
    low_all,
    low_total,
    low_rows,
    up_out,
    up_all,
    up_total,
    up_rows,
    off_out,
    off_all,
    off_total,
    off_rows,
    plane_levels,
    row_levels,
    table,
    products,
    select_first,
    select_second,
    select_third,
    select_extra,
    outgoing,
    arrived,
    extra_out,
    extra_in,
    load_sem,
    y_send,
    y_recv,
    x_send,
    x_recv,
    v_send,
    v_recv,
):
    loads = []
    for number, (source, target) in enumerate(
        (
            (diag_hbm, diag_ref),
            (lower_hbm, lower_ref),
            (rhs_hbm, rhs_ref),
            (upper_hbm, upper_ref),
            (owner_hbm, owner_ref),
            (count_hbm, count_ref),
            (weight_hbm, weight_ref),
            (index_hbm, index_ref),
        )
    ):
        load = pltpu.make_async_copy(source, target, load_sem.at[number])
        load.start()
        loads.append(load)
    me = lax.axis_index("valve")
    blocks = BLOCKS
    bulk = lax.axis_index("bulk")
    my_x = bulk // NY
    my_y = bulk % NY

    def y_peer(step):
        return {"bulk": my_x * NY + (my_y + step) % NY}

    def x_peer(step):
        return {"bulk": ((my_x + step) % nx) * NY + my_y}

    barrier = pltpu.get_barrier_semaphore()
    for step in range(1, NY):
        pl.semaphore_signal(barrier, inc=1, device_id=y_peer(step), device_id_type=MESH)
    for step in range(1, nx):
        pl.semaphore_signal(barrier, inc=1, device_id=x_peer(step), device_id_type=MESH)

    for step in range(1, nv):
        pl.semaphore_signal(barrier, inc=1, device_id={"valve": (me + step) % nv}, device_id_type=MESH)

    def place(ref, index, rows):
        return ref.at[pl.ds(pl.multiple_of(index * rows, 8), rows), :]

    def send_y(stage, source, target, rows):
        copies = []
        for step in (4, 3, 5, 2, 6, 1, 7):
            copy = pltpu.make_async_remote_copy(
                src_ref=source,
                dst_ref=place(target, my_y, rows),
                send_sem=y_send.at[stage, step - 1],
                recv_sem=y_recv.at[stage, step - 1],
                device_id=y_peer(step),
                device_id_type=MESH,
            )
            copy.start()
            copies.append(copy)
        return copies

    def send_x(stage, source, target, rows):
        copies = []
        for step in range(1, nx):
            copy = pltpu.make_async_remote_copy(
                src_ref=source,
                dst_ref=place(target, my_x, rows),
                send_sem=x_send.at[stage, step - 1],
                recv_sem=x_recv.at[stage, step - 1],
                device_id=x_peer(step),
                device_id_type=MESH,
            )
            copy.start()
            copies.append(copy)
        return copies

    def arrive(copies):
        for copy in copies:
            copy.wait_recv()

    def put(ref, first, value, row):
        for index in range(value.shape[0]):
            ref[first + index : first + index + 1, :] = value[index, row : row + 1, :]

    def gathered(ref, first, count, stride):
        return jnp.stack([ref[pl.ds(first + index, 8, stride=stride), :] for index in range(count)])

    for load in loads[:3]:
        load.wait()
    diag = diag_ref[...]
    low_matrices, low_offsets = forward_scan(-compose(diag, lower_ref[...]), apply(diag, rhs_ref[...]))
    put(low_out, 0, low_matrices.reshape(25, PLANES, CELLS), PLANES - 1)
    put(low_out, 25, low_offsets, PLANES - 1)
    place(low_all, my_y, ROWS)[...] = low_out[...]
    pl.semaphore_wait(barrier, NY + nx + nv - 3)
    low_y = send_y(0, low_out, low_all, ROWS)

    loads[3].wait()
    up_matrices = backward_matrices(-compose(diag, upper_ref[...]), plane_levels)
    put(up_out, 0, up_matrices.reshape(25, PLANES, CELLS), 0)
    place(up_all, my_y, ROWS)[...] = up_out[...]
    up_y = send_y(1, up_out, up_all, ROWS)

    for load in loads[4:]:
        load.wait()
    lane = lax.broadcasted_iota(jnp.int32, (1, CELLS), 1)
    block_of = lane >> 3
    owner = jnp.zeros((1, CELLS), jnp.int32)
    for block in range(blocks):
        owner = jnp.where(block_of == block, owner_ref[0, block], owner)
    rank = jnp.zeros((1, CELLS), jnp.int32)
    for earlier in range(blocks):
        same = (owner == owner_ref[0, earlier]) & (block_of > earlier)
        rank = rank + jnp.where(same, 1, 0)
    goal = owner * CAPACITY + rank
    line = lax.broadcasted_iota(jnp.int32, (nv * 8, CELLS), 0)
    for tile, (selection, first, last) in enumerate(
        ((select_first, 0, 2), (select_second, 1, 4), (select_third, 3, 5))
    ):
        number = tile * 8 + (line & 7)
        component = (number * 13) >> 6
        wanted = (line >> 3) * CAPACITY + number - component * CAPACITY
        for c in range(first, last):
            hit = (component == c) & (wanted == goal)
            selection[:, (c - first) * CELLS : (c - first + 1) * CELLS] = jnp.where(hit, 1.0, 0.0).astype(F32)
    wanted = lax.broadcasted_iota(jnp.int32, (nv, CELLS), 0) * CAPACITY + CAPACITY - 1
    select_extra[...] = jnp.where(wanted == goal, 1.0, 0.0).astype(F32)
    for block in range(blocks):
        weight_ref[block] = jnp.where(lane < count_ref[0, block], weight_ref[block], 0.0)

    arrive(low_y)
    row_matrices, row_offsets = forward_scan(
        gathered(low_all, 0, 25, ROWS).reshape(5, 5, 8, CELLS), gathered(low_all, 25, 5, ROWS)
    )
    put(low_total, 0, row_matrices.reshape(25, 8, CELLS), 7)
    put(low_total, 25, row_offsets, 7)
    low_x = send_x(0, low_total, low_rows, ROWS)

    arrive(up_y)
    row_up = backward_matrices(gathered(up_all, 0, 25, ROWS).reshape(5, 5, 8, CELLS), row_levels)
    put(up_total, 0, row_up.reshape(25, 8, CELLS), 0)
    up_x = send_x(1, up_total, up_rows, ROWS)

    place(low_rows, my_x, ROWS)[...] = low_total[...]
    place(up_rows, my_x, ROWS)[...] = up_total[...]

    def chain(rows, offsets_of, order, passes):
        state = [jnp.zeros((1, CELLS), F32) for _ in range(5)]
        for x in order:
            offsets = offsets_of(x)
            new_state = []
            for a in range(5):
                value = offsets[a]
                for b in range(5):
                    at = x * ROWS + a * 5 + b
                    value = value + rows[at : at + 1, :] * state[b]
                new_state.append(value)
            keep = passes(x)
            state = [jnp.where(keep, new, old) for new, old in zip(new_state, state)]
        return jnp.stack([jnp.broadcast_to(value, (8, CELLS)) for value in state])

    arrive(low_x)
    entering = chain(
        low_rows,
        lambda x: [low_rows[x * ROWS + 25 + a : x * ROWS + 26 + a, :] for a in range(5)],
        range(nx - 1),
        lambda x: x < my_x,
    )
    leaving = row_offsets + apply(row_matrices, entering)
    incoming = jnp.where(my_y == 0, entering, picked_row(leaving, my_y - 1))
    starred = low_offsets + apply(low_matrices, incoming)

    partial = backward_offsets(plane_levels, starred)
    put(off_out, 0, partial, 0)
    off_y = send_y(2, off_out, off_all, 8)
    place(off_all, my_y, 8)[...] = off_out[...]
    arrive(up_x)
    arrive(off_y)
    row_partial = backward_offsets(row_levels, gathered(off_all, 0, 5, 8))
    put(off_total, 0, row_partial, 0)
    off_x = send_x(2, off_total, off_rows, 8)
    place(off_rows, my_x, 8)[...] = off_total[...]
    arrive(off_x)
    entering = chain(
        up_rows,
        lambda x: [off_rows[x * 8 + a : x * 8 + a + 1, :] for a in range(5)],
        range(nx - 1, 0, -1),
        lambda x: x > my_x,
    )
    leaving = row_partial + apply(row_up, entering)
    incoming = jnp.where(my_y == NY - 1, entering, picked_row(leaving, my_y + 1))
    update = partial + apply(up_matrices, incoming)
    update_ref[...] = update
    for c in range(5):
        for plane in range(PLANES):
            table[c, plane] = jnp.broadcast_to(update[c, plane : plane + 1, :], (8, CELLS))

    def interpolate(components):
        def step(block, carry):
            donors = index_ref[block]
            weights = weight_ref[block]
            cell = donors & (CELLS - 1)
            plane_of = donors >> 7
            here = [plane_of == plane for plane in range(PLANES)]
            for c in components:
                picked = jnp.take_along_axis(table[c, 0], cell, axis=1, mode="promise_in_bounds")
                for plane in range(1, PLANES):
                    other = jnp.take_along_axis(table[c, plane], cell, axis=1, mode="promise_in_bounds")
                    picked = jnp.where(here[plane], other, picked)
                products[c, pl.ds(pl.multiple_of(block * 8, 8), 8), :] = weights * picked
            return carry

        lax.fori_loop(0, blocks, step, 0, unroll=2)

    def selected(selection, first, last):
        total = None
        for c in range(first, last):
            part = jnp.dot(
                selection[:, (c - first) * CELLS : (c - first + 1) * CELLS],
                products[c],
                precision=lax.Precision.HIGHEST,
                preferred_element_type=F32,
            )
            total = part if total is None else total + part
        return total

    def send_v(stage, source_of, target_of):
        copies = []
        for step in sorted(range(1, nv), key=lambda step: -min(step, nv - step)):
            peer = (me + step) % nv
            copy = pltpu.make_async_remote_copy(
                src_ref=source_of(peer),
                dst_ref=target_of(me),
                send_sem=v_send.at[stage, step - 1],
                recv_sem=v_recv.at[stage, step - 1],
                device_id={"valve": peer},
                device_id_type=MESH,
            )
            copy.start()
            copies.append(copy)
        return copies

    def exchange(tile, selection, first, last):
        outgoing[tile] = selected(selection, first, last).reshape(nv, 8, POINTS)
        copies = send_v(tile, lambda peer: outgoing.at[tile, peer], lambda mine: arrived.at[tile, mine])
        arrived[tile, me] = outgoing[tile, me]
        return copies

    sent = []
    interpolate((0, 1))
    sent += exchange(0, select_first, 0, 2)
    interpolate((2, 3))
    sent += exchange(1, select_second, 1, 4)
    interpolate((4,))
    sent += exchange(2, select_third, 3, 5)
    extra = selected(select_extra, 4, 5)
    for device in range(nv):
        extra_out[device] = extra[device : device + 1, :]
    sent += send_v(3, lambda peer: extra_out.at[peer], lambda mine: extra_in.at[mine])
    extra_in[me] = extra_out[me]

    arrive(sent)
    for source in range(nv):
        base = source * CAPACITY
        for c in range(5):
            slot = 0
            while slot < CAPACITY:
                number = c * CAPACITY + slot
                if number == 24:
                    fringe_ref[c, base + slot : base + slot + 1, :] = extra_in[source]
                    break
                row = number % 8
                count = min(CAPACITY - slot, 8 - row)
                fringe_ref[c, base + slot : base + slot + count, :] = arrived[number // 8, source, row : row + count, :]
                slot += count

    for copies in (low_y, up_y, low_x, up_x, off_y, off_x, sent):
        for copy in copies:
            copy.wait_send()


def whole(nx, nv, rhs, diag, lower, upper, index, weight, count, owner):
    hbm = pl.BlockSpec(memory_space=pl.ANY)
    vmem = pl.BlockSpec(memory_space=VMEM)
    return pl.pallas_call(
        functools.partial(whole_kernel, nx, nv),
        out_shape=(
            jax.ShapeDtypeStruct((5, PLANES, CELLS), F32),
            jax.ShapeDtypeStruct((5, nv * CAPACITY, POINTS), F32),
        ),
        in_specs=[hbm] * 8,
        out_specs=(vmem, vmem),
        scratch_shapes=[
            VMEM((5, PLANES, CELLS), F32),
            VMEM((5, 5, PLANES, CELLS), F32),
            VMEM((5, 5, PLANES, CELLS), F32),
            VMEM((5, 5, PLANES, CELLS), F32),
            VMEM((BLOCKS, 8, POINTS), jnp.int32),
            VMEM((BLOCKS, 8, POINTS), F32),
            pltpu.SMEM((1, BLOCKS), jnp.int32),
            pltpu.SMEM((1, BLOCKS), jnp.int32),
            VMEM((ROWS, CELLS), F32),
            VMEM((NY * ROWS, CELLS), F32),
            VMEM((ROWS, CELLS), F32),
            VMEM((nx * ROWS, CELLS), F32),
            VMEM((ROWS, CELLS), F32),
            VMEM((NY * ROWS, CELLS), F32),
            VMEM((ROWS, CELLS), F32),
            VMEM((nx * ROWS, CELLS), F32),
            VMEM((8, CELLS), F32),
            VMEM((NY * 8, CELLS), F32),
            VMEM((8, CELLS), F32),
            VMEM((nx * 8, CELLS), F32),
            VMEM((3, 5, 5, 8, CELLS), F32),
            VMEM((3, 5, 5, 8, CELLS), F32),
            VMEM((5, PLANES, 8, CELLS), F32),
            VMEM((5, BLOCKS * 8, POINTS), F32),
            VMEM((nv * 8, 2 * CELLS), F32),
            VMEM((nv * 8, 3 * CELLS), F32),
            VMEM((nv * 8, 2 * CELLS), F32),
            VMEM((nv, CELLS), F32),
            VMEM((3, nv, 8, POINTS), F32),
            VMEM((3, nv, 8, POINTS), F32),
            VMEM((nv, 1, POINTS), F32),
            VMEM((nv, 1, POINTS), F32),
            pltpu.SemaphoreType.DMA((8,)),
            pltpu.SemaphoreType.DMA((3, NY - 1)),
            pltpu.SemaphoreType.DMA((3, NY - 1)),
            pltpu.SemaphoreType.DMA((3, nx - 1)),
            pltpu.SemaphoreType.DMA((3, nx - 1)),
            pltpu.SemaphoreType.DMA((4, nv - 1)),
            pltpu.SemaphoreType.DMA((4, nv - 1)),
        ],
        compiler_params=pltpu.CompilerParams(collective_id=0, has_side_effects=True),
    )(rhs, diag, lower, upper, index, weight, count, owner)


def solution(mesh):
    nx = mesh.shape["bulk"] // NY
    nv = mesh.shape["valve"]

    def body(rhs, diag, lower, upper, index, weight, count, owner):
        update, rows = whole(nx, nv, rhs, diag, lower, upper, index[0], weight[0], count, owner)
        return update, jnp.transpose(rows, (1, 0, 2))[None]

    in_specs = (
        P(None, "bulk", "valve"),
        P(None, None, "bulk", "valve"),
        P(None, None, "bulk", "valve"),
        P(None, None, "bulk", "valve"),
        P("bulk", "valve", None, None),
        P("bulk", "valve", None, None),
        P("bulk", "valve"),
        P("bulk", "valve"),
    )
    out_specs = (P(None, "bulk", "valve"), P("bulk", "valve", None, None))
    return jax.shard_map(body, mesh=mesh, in_specs=in_specs, out_specs=out_specs, check_vma=False)
```

```python
import functools

import jax
import jax.numpy as jnp
from jax import lax
from jax.experimental import pallas as pl
from jax.experimental.pallas import tpu as pltpu
from jax.sharding import PartitionSpec as P

NY = 8
PLANES = 8
CELLS = 128
POINTS = 128
CAPACITY = 5
ROWS = 32
BLOCKS = 16
MESH = pl.DeviceIdType.MESH
VMEM = pltpu.VMEM
F32 = jnp.float32


def compose(left, right):
    total = left[:, 0][:, None] * right[0][None]
    for c in range(1, 5):
        total = total + left[:, c][:, None] * right[c][None]
    return total


def apply(matrices, vectors):
    total = matrices[:, 0] * vectors[0][None]
    for c in range(1, 5):
        total = total + matrices[:, c] * vectors[c][None]
    return total


def shifted(value, amount):
    shape = value.shape
    flat = value.reshape((-1,) + shape[-2:])
    return pltpu.roll(flat, amount % shape[-2], 1).reshape(shape)


def forward_scan(matrices, offsets):
    row = lax.broadcasted_iota(jnp.int32, (8, CELLS), 0)
    for step in (1, 2, 4):
        live = row >= step
        new_offsets = offsets + apply(matrices, shifted(offsets, step))
        new_matrices = compose(matrices, shifted(matrices, step))
        offsets = jnp.where(live[None], new_offsets, offsets)
        matrices = jnp.where(live[None, None], new_matrices, matrices)
    return matrices, offsets


def backward_matrices(matrices, levels_ref):
    row = lax.broadcasted_iota(jnp.int32, (8, CELLS), 0)
    for level, step in enumerate((1, 2, 4)):
        live = row < 8 - step
        levels_ref[level] = jnp.where(live[None, None], matrices, 0.0)
        matrices = jnp.where(live[None, None], compose(matrices, shifted(matrices, -step)), matrices)
    return matrices


def backward_offsets(levels_ref, offsets):
    for level, step in enumerate((1, 2, 4)):
        offsets = offsets + apply(levels_ref[level], shifted(offsets, -step))
    return offsets


def picked_row(values, index):
    row = lax.broadcasted_iota(jnp.int32, (8, CELLS), 0)
    kept = jnp.where((row == index)[None], values, 0.0)
    for step in (1, 2, 4):
        kept = kept + shifted(kept, step)
    return kept


def whole_kernel(
    nx,
    nv,
    rhs_hbm,
    diag_hbm,
    lower_hbm,
    upper_hbm,
    index_hbm,
    weight_hbm,
    count_hbm,
    owner_hbm,
    update_ref,
    fringe_ref,
    rhs_ref,
    diag_ref,
    lower_ref,
    upper_ref,
    index_ref,
    weight_ref,
    count_ref,
    owner_ref,
    low_out,
    low_all,
    low_total,
    low_rows,
    up_out,
    up_all,
    up_total,
    up_rows,
    off_out,
    off_all,
    off_total,
    off_rows,
    plane_levels,
    row_levels,
    table,
    products,
    select_first,
    select_second,
    select_third,
    select_extra,
    outgoing,
    arrived,
    extra_out,
    extra_in,
    load_sem,
    y_send,
    y_recv,
    x_send,
    x_recv,
    v_send,
    v_recv,
):
    loads = []
    for number, (source, target) in enumerate(
        (
            (diag_hbm, diag_ref),
            (lower_hbm, lower_ref),
            (rhs_hbm, rhs_ref),
            (upper_hbm, upper_ref),
            (owner_hbm, owner_ref),
            (count_hbm, count_ref),
            (weight_hbm, weight_ref),
            (index_hbm, index_ref),
        )
    ):
        load = pltpu.make_async_copy(source, target, load_sem.at[number])
        load.start()
        loads.append(load)
    me = lax.axis_index("valve")
    blocks = BLOCKS
    bulk = lax.axis_index("bulk")
    my_x = bulk // NY
    my_y = bulk % NY

    def y_peer(step):
        return {"bulk": my_x * NY + (my_y + step) % NY}

    def x_peer(step):
        return {"bulk": ((my_x + step) % nx) * NY + my_y}

    barrier = pltpu.get_barrier_semaphore()
    for step in range(1, NY):
        pl.semaphore_signal(barrier, inc=1, device_id=y_peer(step), device_id_type=MESH)
    for step in range(1, nx):
        pl.semaphore_signal(barrier, inc=1, device_id=x_peer(step), device_id_type=MESH)

    for step in range(1, nv):
        pl.semaphore_signal(barrier, inc=1, device_id={"valve": (me + step) % nv}, device_id_type=MESH)

    def place(ref, index, rows):
        return ref.at[pl.ds(pl.multiple_of(index * rows, 8), rows), :]

    def send_y(stage, source, target, rows):
        copies = []
        for step in (4, 3, 5, 2, 6, 1, 7):
            copy = pltpu.make_async_remote_copy(
                src_ref=source,
                dst_ref=place(target, my_y, rows),
                send_sem=y_send.at[stage, step - 1],
                recv_sem=y_recv.at[stage, step - 1],
                device_id=y_peer(step),
                device_id_type=MESH,
            )
            copy.start()
            copies.append(copy)
        return copies

    def send_x(stage, source, target, rows):
        copies = []
        for step in range(1, nx):
            copy = pltpu.make_async_remote_copy(
                src_ref=source,
                dst_ref=place(target, my_x, rows),
                send_sem=x_send.at[stage, step - 1],
                recv_sem=x_recv.at[stage, step - 1],
                device_id=x_peer(step),
                device_id_type=MESH,
            )
            copy.start()
            copies.append(copy)
        return copies

    def arrive(copies):
        for copy in copies:
            copy.wait_recv()

    def put(ref, first, value, row):
        for index in range(value.shape[0]):
            ref[first + index : first + index + 1, :] = value[index, row : row + 1, :]

    def gathered(ref, first, count, stride):
        return jnp.stack([ref[pl.ds(first + index, 8, stride=stride), :] for index in range(count)])

    for load in loads[:3]:
        load.wait()
    diag = diag_ref[...]
    low_matrices, low_offsets = forward_scan(-compose(diag, lower_ref[...]), apply(diag, rhs_ref[...]))
    put(low_out, 0, low_matrices.reshape(25, PLANES, CELLS), PLANES - 1)
    put(low_out, 25, low_offsets, PLANES - 1)
    place(low_all, my_y, ROWS)[...] = low_out[...]
    pl.semaphore_wait(barrier, NY + nx + nv - 3)
    low_y = send_y(0, low_out, low_all, ROWS)

    loads[3].wait()
    up_matrices = backward_matrices(-compose(diag, upper_ref[...]), plane_levels)
    put(up_out, 0, up_matrices.reshape(25, PLANES, CELLS), 0)
    place(up_all, my_y, ROWS)[...] = up_out[...]

    for load in loads[4:]:
        load.wait()
    lane = lax.broadcasted_iota(jnp.int32, (1, CELLS), 1)
    block_of = lane >> 3
    owner = jnp.zeros((1, CELLS), jnp.int32)
    for block in range(blocks):
        owner = jnp.where(block_of == block, owner_ref[0, block], owner)
    rank = jnp.zeros((1, CELLS), jnp.int32)
    for earlier in range(blocks):
        same = (owner == owner_ref[0, earlier]) & (block_of > earlier)
        rank = rank + jnp.where(same, 1, 0)
    goal = owner * CAPACITY + rank
    line = lax.broadcasted_iota(jnp.int32, (nv * 8, CELLS), 0)
    for tile, (selection, first, last) in enumerate(
        ((select_first, 0, 2), (select_second, 1, 4), (select_third, 3, 5))
    ):
        number = tile * 8 + (line & 7)
        component = (number * 13) >> 6
        wanted = (line >> 3) * CAPACITY + number - component * CAPACITY
        for c in range(first, last):
            hit = (component == c) & (wanted == goal)
            selection[:, (c - first) * CELLS : (c - first + 1) * CELLS] = jnp.where(hit, 1.0, 0.0).astype(F32)
    wanted = lax.broadcasted_iota(jnp.int32, (nv, CELLS), 0) * CAPACITY + CAPACITY - 1
    select_extra[...] = jnp.where(wanted == goal, 1.0, 0.0).astype(F32)
    for block in range(blocks):
        weight_ref[block] = jnp.where(lane < count_ref[0, block], weight_ref[block], 0.0)

    arrive(low_y)
    up_y = send_y(1, up_out, up_all, ROWS)
    row_matrices, row_offsets = forward_scan(
        gathered(low_all, 0, 25, ROWS).reshape(5, 5, 8, CELLS), gathered(low_all, 25, 5, ROWS)
    )
    put(low_total, 0, row_matrices.reshape(25, 8, CELLS), 7)
    put(low_total, 25, row_offsets, 7)
    low_x = send_x(0, low_total, low_rows, ROWS)

    arrive(up_y)
    row_up = backward_matrices(gathered(up_all, 0, 25, ROWS).reshape(5, 5, 8, CELLS), row_levels)
    put(up_total, 0, row_up.reshape(25, 8, CELLS), 0)
    up_x = send_x(1, up_total, up_rows, ROWS)

    place(low_rows, my_x, ROWS)[...] = low_total[...]
    place(up_rows, my_x, ROWS)[...] = up_total[...]

    def chain(rows, offsets_of, order, passes):
        state = [jnp.zeros((1, CELLS), F32) for _ in range(5)]
        for x in order:
            offsets = offsets_of(x)
            new_state = []
            for a in range(5):
                value = offsets[a]
                for b in range(5):
                    at = x * ROWS + a * 5 + b
                    value = value + rows[at : at + 1, :] * state[b]
                new_state.append(value)
            keep = passes(x)
            state = [jnp.where(keep, new, old) for new, old in zip(new_state, state)]
        return jnp.stack([jnp.broadcast_to(value, (8, CELLS)) for value in state])

    arrive(low_x)
    entering = chain(
        low_rows,
        lambda x: [low_rows[x * ROWS + 25 + a : x * ROWS + 26 + a, :] for a in range(5)],
        range(nx - 1),
        lambda x: x < my_x,
    )
    leaving = row_offsets + apply(row_matrices, entering)
    incoming = jnp.where(my_y == 0, entering, picked_row(leaving, my_y - 1))
    starred = low_offsets + apply(low_matrices, incoming)

    partial = backward_offsets(plane_levels, starred)
    put(off_out, 0, partial, 0)
    off_y = send_y(2, off_out, off_all, 8)
    place(off_all, my_y, 8)[...] = off_out[...]
    arrive(up_x)
    arrive(off_y)
    row_partial = backward_offsets(row_levels, gathered(off_all, 0, 5, 8))
    put(off_total, 0, row_partial, 0)
    off_x = send_x(2, off_total, off_rows, 8)
    place(off_rows, my_x, 8)[...] = off_total[...]
    arrive(off_x)
    entering = chain(
        up_rows,
        lambda x: [off_rows[x * 8 + a : x * 8 + a + 1, :] for a in range(5)],
        range(nx - 1, 0, -1),
        lambda x: x > my_x,
    )
    leaving = row_partial + apply(row_up, entering)
    incoming = jnp.where(my_y == NY - 1, entering, picked_row(leaving, my_y + 1))
    update = partial + apply(up_matrices, incoming)
    update_ref[...] = update
    for c in range(5):
        for plane in range(PLANES):
            table[c, plane] = jnp.broadcast_to(update[c, plane : plane + 1, :], (8, CELLS))

    def interpolate(components):
        def step(block, carry):
            donors = index_ref[block]
            weights = weight_ref[block]
            cell = donors & (CELLS - 1)
            plane_of = donors >> 7
            here = [plane_of == plane for plane in range(PLANES)]
            for c in components:
                picked = jnp.take_along_axis(table[c, 0], cell, axis=1, mode="promise_in_bounds")
                for plane in range(1, PLANES):
                    other = jnp.take_along_axis(table[c, plane], cell, axis=1, mode="promise_in_bounds")
                    picked = jnp.where(here[plane], other, picked)
                products[c, pl.ds(pl.multiple_of(block * 8, 8), 8), :] = weights * picked
            return carry

        lax.fori_loop(0, blocks, step, 0, unroll=2)

    def selected(selection, first, last):
        total = None
        for c in range(first, last):
            part = jnp.dot(
                selection[:, (c - first) * CELLS : (c - first + 1) * CELLS],
                products[c],
                precision=lax.Precision.HIGHEST,
                preferred_element_type=F32,
            )
            total = part if total is None else total + part
        return total

    def send_v(stage, source_of, target_of):
        copies = []
        for step in sorted(range(1, nv), key=lambda step: -min(step, nv - step)):
            peer = (me + step) % nv
            copy = pltpu.make_async_remote_copy(
                src_ref=source_of(peer),
                dst_ref=target_of(me),
                send_sem=v_send.at[stage, step - 1],
                recv_sem=v_recv.at[stage, step - 1],
                device_id={"valve": peer},
                device_id_type=MESH,
            )
            copy.start()
            copies.append(copy)
        return copies

    def exchange(tile, selection, first, last):
        outgoing[tile] = selected(selection, first, last).reshape(nv, 8, POINTS)
        copies = send_v(tile, lambda peer: outgoing.at[tile, peer], lambda mine: arrived.at[tile, mine])
        arrived[tile, me] = outgoing[tile, me]
        return copies

    sent = []
    interpolate((0, 1))
    sent += exchange(0, select_first, 0, 2)
    interpolate((2, 3))
    sent += exchange(1, select_second, 1, 4)
    interpolate((4,))
    sent += exchange(2, select_third, 3, 5)
    extra = selected(select_extra, 4, 5)
    for device in range(nv):
        extra_out[device] = extra[device : device + 1, :]
    sent += send_v(3, lambda peer: extra_out.at[peer], lambda mine: extra_in.at[mine])
    extra_in[me] = extra_out[me]

    arrive(sent)
    for source in range(nv):
        base = source * CAPACITY
        for c in range(5):
            slot = 0
            while slot < CAPACITY:
                number = c * CAPACITY + slot
                if number == 24:
                    fringe_ref[c, base + slot : base + slot + 1, :] = extra_in[source]
                    break
                row = number % 8
                count = min(CAPACITY - slot, 8 - row)
                fringe_ref[c, base + slot : base + slot + count, :] = arrived[number // 8, source, row : row + count, :]
                slot += count

    for copies in (low_y, up_y, low_x, up_x, off_y, off_x, sent):
        for copy in copies:
            copy.wait_send()


def whole(nx, nv, rhs, diag, lower, upper, index, weight, count, owner):
    hbm = pl.BlockSpec(memory_space=pl.ANY)
    vmem = pl.BlockSpec(memory_space=VMEM)
    return pl.pallas_call(
        functools.partial(whole_kernel, nx, nv),
        out_shape=(
            VMEM((5, PLANES, CELLS), F32),
            VMEM((5, nv * CAPACITY, POINTS), F32),
        ),
        in_specs=[hbm] * 8,
        out_specs=(vmem, vmem),
        scratch_shapes=[
            VMEM((5, PLANES, CELLS), F32),
            VMEM((5, 5, PLANES, CELLS), F32),
            VMEM((5, 5, PLANES, CELLS), F32),
            VMEM((5, 5, PLANES, CELLS), F32),
            VMEM((BLOCKS, 8, POINTS), jnp.int32),
            VMEM((BLOCKS, 8, POINTS), F32),
            pltpu.SMEM((1, BLOCKS), jnp.int32),
            pltpu.SMEM((1, BLOCKS), jnp.int32),
            VMEM((ROWS, CELLS), F32),
            VMEM((NY * ROWS, CELLS), F32),
            VMEM((ROWS, CELLS), F32),
            VMEM((nx * ROWS, CELLS), F32),
            VMEM((ROWS, CELLS), F32),
            VMEM((NY * ROWS, CELLS), F32),
            VMEM((ROWS, CELLS), F32),
            VMEM((nx * ROWS, CELLS), F32),
            VMEM((8, CELLS), F32),
            VMEM((NY * 8, CELLS), F32),
            VMEM((8, CELLS), F32),
            VMEM((nx * 8, CELLS), F32),
            VMEM((3, 5, 5, 8, CELLS), F32),
            VMEM((3, 5, 5, 8, CELLS), F32),
            VMEM((5, PLANES, 8, CELLS), F32),
            VMEM((5, BLOCKS * 8, POINTS), F32),
            VMEM((nv * 8, 2 * CELLS), F32),
            VMEM((nv * 8, 3 * CELLS), F32),
            VMEM((nv * 8, 2 * CELLS), F32),
            VMEM((nv, CELLS), F32),
            VMEM((3, nv, 8, POINTS), F32),
            VMEM((3, nv, 8, POINTS), F32),
            VMEM((nv, 1, POINTS), F32),
            VMEM((nv, 1, POINTS), F32),
            pltpu.SemaphoreType.DMA((8,)),
            pltpu.SemaphoreType.DMA((3, NY - 1)),
            pltpu.SemaphoreType.DMA((3, NY - 1)),
            pltpu.SemaphoreType.DMA((3, nx - 1)),
            pltpu.SemaphoreType.DMA((3, nx - 1)),
            pltpu.SemaphoreType.DMA((4, nv - 1)),
            pltpu.SemaphoreType.DMA((4, nv - 1)),
        ],
        compiler_params=pltpu.CompilerParams(collective_id=0, has_side_effects=True),
    )(rhs, diag, lower, upper, index, weight, count, owner)


def solution(mesh):
    nx = mesh.shape["bulk"] // NY
    nv = mesh.shape["valve"]

    def body(rhs, diag, lower, upper, index, weight, count, owner):
        update, rows = whole(nx, nv, rhs, diag, lower, upper, index[0], weight[0], count, owner)
        return update, jnp.transpose(rows, (1, 0, 2))[None]

    in_specs = (
        P(None, "bulk", "valve"),
        P(None, None, "bulk", "valve"),
        P(None, None, "bulk", "valve"),
        P(None, None, "bulk", "valve"),
        P("bulk", "valve", None, None),
        P("bulk", "valve", None, None),
        P("bulk", "valve"),
        P("bulk", "valve"),
    )
    out_specs = (P(None, "bulk", "valve"), P("bulk", "valve", None, None))
    return jax.shard_map(body, mesh=mesh, in_specs=in_specs, out_specs=out_specs, check_vma=False)
```

```python
import functools

import jax
import jax.numpy as jnp
from jax import lax
from jax.experimental import pallas as pl
from jax.experimental.pallas import tpu as pltpu
from jax.sharding import PartitionSpec as P

NY = 8
PLANES = 8
CELLS = 128
POINTS = 128
CAPACITY = 5
ROWS = 32
BLOCKS = 16
MESH = pl.DeviceIdType.MESH
VMEM = pltpu.VMEM
F32 = jnp.float32


def compose(left, right):
    total = left[:, 0][:, None] * right[0][None]
    for c in range(1, 5):
        total = total + left[:, c][:, None] * right[c][None]
    return total


def apply(matrices, vectors):
    total = matrices[:, 0] * vectors[0][None]
    for c in range(1, 5):
        total = total + matrices[:, c] * vectors[c][None]
    return total


def shifted(value, amount):
    shape = value.shape
    flat = value.reshape((-1,) + shape[-2:])
    return pltpu.roll(flat, amount % shape[-2], 1).reshape(shape)


def forward_scan(matrices, offsets):
    row = lax.broadcasted_iota(jnp.int32, (8, CELLS), 0)
    for step in (1, 2, 4):
        live = row >= step
        new_offsets = offsets + apply(matrices, shifted(offsets, step))
        new_matrices = compose(matrices, shifted(matrices, step))
        offsets = jnp.where(live[None], new_offsets, offsets)
        matrices = jnp.where(live[None, None], new_matrices, matrices)
    return matrices, offsets


def backward_matrices(matrices, levels_ref):
    row = lax.broadcasted_iota(jnp.int32, (8, CELLS), 0)
    for level, step in enumerate((1, 2, 4)):
        live = row < 8 - step
        levels_ref[level] = jnp.where(live[None, None], matrices, 0.0)
        matrices = jnp.where(live[None, None], compose(matrices, shifted(matrices, -step)), matrices)
    return matrices


def backward_offsets(levels_ref, offsets):
    for level, step in enumerate((1, 2, 4)):
        offsets = offsets + apply(levels_ref[level], shifted(offsets, -step))
    return offsets


def picked_row(values, index):
    row = lax.broadcasted_iota(jnp.int32, (8, CELLS), 0)
    kept = jnp.where((row == index)[None], values, 0.0)
    for step in (1, 2, 4):
        kept = kept + shifted(kept, step)
    return kept


def whole_kernel(
    nx,
    nv,
    rhs_hbm,
    diag_hbm,
    lower_hbm,
    upper_hbm,
    index_hbm,
    weight_hbm,
    count_hbm,
    owner_hbm,
    update_ref,
    fringe_ref,
    rhs_ref,
    diag_ref,
    lower_ref,
    upper_ref,
    index_ref,
    weight_ref,
    count_ref,
    owner_ref,
    low_out,
    low_all,
    low_total,
    low_rows,
    up_out,
    up_all,
    up_total,
    up_rows,
    off_out,
    off_all,
    off_total,
    off_rows,
    plane_levels,
    row_levels,
    table,
    products,
    select_first,
    select_second,
    select_third,
    select_extra,
    outgoing,
    arrived,
    extra_out,
    extra_in,
    load_sem,
    y_send,
    y_recv,
    x_send,
    x_recv,
    v_send,
    v_recv,
):
    loads = []
    for number, (source, target) in enumerate(
        (
            (diag_hbm, diag_ref),
            (lower_hbm, lower_ref),
            (rhs_hbm, rhs_ref),
            (upper_hbm, upper_ref),
            (owner_hbm, owner_ref),
            (count_hbm, count_ref),
            (weight_hbm, weight_ref),
            (index_hbm, index_ref),
        )
    ):
        load = pltpu.make_async_copy(source, target, load_sem.at[number])
        load.start()
        loads.append(load)
    me = lax.axis_index("valve")
    blocks = BLOCKS
    bulk = lax.axis_index("bulk")
    my_x = bulk // NY
    my_y = bulk % NY

    def y_peer(step):
        return {"bulk": my_x * NY + (my_y + step) % NY}

    def x_peer(step):
        return {"bulk": ((my_x + step) % nx) * NY + my_y}

    barrier = pltpu.get_barrier_semaphore()
    for step in range(1, NY):
        pl.semaphore_signal(barrier, inc=1, device_id=y_peer(step), device_id_type=MESH)
    for step in range(1, nx):
        pl.semaphore_signal(barrier, inc=1, device_id=x_peer(step), device_id_type=MESH)

    for step in range(1, nv):
        pl.semaphore_signal(barrier, inc=1, device_id={"valve": (me + step) % nv}, device_id_type=MESH)

    def place(ref, index, rows):
        return ref.at[pl.ds(pl.multiple_of(index * rows, 8), rows), :]

    def send_y(stage, source, target, rows):
        copies = []
        for step in (4, 3, 5, 2, 6, 1, 7):
            copy = pltpu.make_async_remote_copy(
                src_ref=source,
                dst_ref=place(target, my_y, rows),
                send_sem=y_send.at[stage, step - 1],
                recv_sem=y_recv.at[stage, step - 1],
                device_id=y_peer(step),
                device_id_type=MESH,
            )
            copy.start()
            copies.append(copy)
        return copies

    def send_x(stage, source, target, rows):
        copies = []
        for step in range(1, nx):
            copy = pltpu.make_async_remote_copy(
                src_ref=source,
                dst_ref=place(target, my_x, rows),
                send_sem=x_send.at[stage, step - 1],
                recv_sem=x_recv.at[stage, step - 1],
                device_id=x_peer(step),
                device_id_type=MESH,
            )
            copy.start()
            copies.append(copy)
        return copies

    def arrive(copies):
        for copy in copies:
            copy.wait_recv()

    def put(ref, first, value, row):
        for index in range(value.shape[0]):
            ref[first + index : first + index + 1, :] = value[index, row : row + 1, :]

    def gathered(ref, first, count, stride):
        return jnp.stack([ref[pl.ds(first + index, 8, stride=stride), :] for index in range(count)])

    for load in loads[:3]:
        load.wait()
    diag = diag_ref[...]
    low_matrices, low_offsets = forward_scan(-compose(diag, lower_ref[...]), apply(diag, rhs_ref[...]))
    put(low_out, 0, low_matrices.reshape(25, PLANES, CELLS), PLANES - 1)
    put(low_out, 25, low_offsets, PLANES - 1)
    place(low_all, my_y, ROWS)[...] = low_out[...]
    pl.semaphore_wait(barrier, NY + nx + nv - 3)
    low_y = send_y(0, low_out, low_all, ROWS)

    loads[3].wait()
    up_matrices = backward_matrices(-compose(diag, upper_ref[...]), plane_levels)
    put(up_out, 0, up_matrices.reshape(25, PLANES, CELLS), 0)
    place(up_all, my_y, ROWS)[...] = up_out[...]

    for load in loads[4:]:
        load.wait()
    lane = lax.broadcasted_iota(jnp.int32, (1, CELLS), 1)
    block_of = lane >> 3
    owner = jnp.zeros((1, CELLS), jnp.int32)
    for block in range(blocks):
        owner = jnp.where(block_of == block, owner_ref[0, block], owner)
    rank = jnp.zeros((1, CELLS), jnp.int32)
    for earlier in range(blocks):
        same = (owner == owner_ref[0, earlier]) & (block_of > earlier)
        rank = rank + jnp.where(same, 1, 0)
    goal = owner * CAPACITY + rank
    line = lax.broadcasted_iota(jnp.int32, (nv * 8, CELLS), 0)
    for tile, (selection, first, last) in enumerate(
        ((select_first, 0, 2), (select_second, 1, 4), (select_third, 3, 5))
    ):
        number = tile * 8 + (line & 7)
        component = (number * 13) >> 6
        wanted = (line >> 3) * CAPACITY + number - component * CAPACITY
        for c in range(first, last):
            hit = (component == c) & (wanted == goal)
            selection[:, (c - first) * CELLS : (c - first + 1) * CELLS] = jnp.where(hit, 1.0, 0.0).astype(F32)
    wanted = lax.broadcasted_iota(jnp.int32, (nv, CELLS), 0) * CAPACITY + CAPACITY - 1
    select_extra[...] = jnp.where(wanted == goal, 1.0, 0.0).astype(F32)
    for block in range(blocks):
        weight_ref[block] = jnp.where(lane < count_ref[0, block], weight_ref[block], 0.0)

    arrive(low_y)
    up_y = send_y(1, up_out, up_all, ROWS)
    row_matrices, row_offsets = forward_scan(
        gathered(low_all, 0, 25, ROWS).reshape(5, 5, 8, CELLS), gathered(low_all, 25, 5, ROWS)
    )
    put(low_total, 0, row_matrices.reshape(25, 8, CELLS), 7)
    put(low_total, 25, row_offsets, 7)
    low_x = send_x(0, low_total, low_rows, ROWS)

    place(low_rows, my_x, ROWS)[...] = low_total[...]

    def chain(rows, offsets_of, order, passes):
        state = [jnp.zeros((1, CELLS), F32) for _ in range(5)]
        for x in order:
            offsets = offsets_of(x)
            new_state = []
            for a in range(5):
                value = offsets[a]
                for b in range(5):
                    at = x * ROWS + a * 5 + b
                    value = value + rows[at : at + 1, :] * state[b]
                new_state.append(value)
            keep = passes(x)
            state = [jnp.where(keep, new, old) for new, old in zip(new_state, state)]
        return jnp.stack([jnp.broadcast_to(value, (8, CELLS)) for value in state])

    arrive(low_x)
    entering = chain(
        low_rows,
        lambda x: [low_rows[x * ROWS + 25 + a : x * ROWS + 26 + a, :] for a in range(5)],
        range(nx - 1),
        lambda x: x < my_x,
    )
    leaving = row_offsets + apply(row_matrices, entering)
    incoming = jnp.where(my_y == 0, entering, picked_row(leaving, my_y - 1))
    starred = low_offsets + apply(low_matrices, incoming)

    partial = backward_offsets(plane_levels, starred)
    put(off_out, 0, partial, 0)
    off_y = send_y(2, off_out, off_all, 8)
    place(off_all, my_y, 8)[...] = off_out[...]

    arrive(up_y)
    row_up = backward_matrices(gathered(up_all, 0, 25, ROWS).reshape(5, 5, 8, CELLS), row_levels)
    put(up_total, 0, row_up.reshape(25, 8, CELLS), 0)
    up_x = send_x(1, up_total, up_rows, ROWS)
    place(up_rows, my_x, ROWS)[...] = up_total[...]

    arrive(off_y)
    row_partial = backward_offsets(row_levels, gathered(off_all, 0, 5, 8))
    put(off_total, 0, row_partial, 0)
    off_x = send_x(2, off_total, off_rows, 8)
    place(off_rows, my_x, 8)[...] = off_total[...]
    arrive(up_x)
    arrive(off_x)
    entering = chain(
        up_rows,
        lambda x: [off_rows[x * 8 + a : x * 8 + a + 1, :] for a in range(5)],
        range(nx - 1, 0, -1),
        lambda x: x > my_x,
    )
    leaving = row_partial + apply(row_up, entering)
    incoming = jnp.where(my_y == NY - 1, entering, picked_row(leaving, my_y + 1))
    update = partial + apply(up_matrices, incoming)
    update_ref[...] = update
    for c in range(5):
        for plane in range(PLANES):
            table[c, plane] = jnp.broadcast_to(update[c, plane : plane + 1, :], (8, CELLS))

    def interpolate(components):
        def step(block, carry):
            donors = index_ref[block]
            weights = weight_ref[block]
            cell = donors & (CELLS - 1)
            plane_of = donors >> 7
            here = [plane_of == plane for plane in range(PLANES)]
            for c in components:
                picked = jnp.take_along_axis(table[c, 0], cell, axis=1, mode="promise_in_bounds")
                for plane in range(1, PLANES):
                    other = jnp.take_along_axis(table[c, plane], cell, axis=1, mode="promise_in_bounds")
                    picked = jnp.where(here[plane], other, picked)
                products[c, pl.ds(pl.multiple_of(block * 8, 8), 8), :] = weights * picked
            return carry

        lax.fori_loop(0, blocks, step, 0, unroll=2)

    def selected(selection, first, last):
        total = None
        for c in range(first, last):
            part = jnp.dot(
                selection[:, (c - first) * CELLS : (c - first + 1) * CELLS],
                products[c],
                precision=lax.Precision.HIGHEST,
                preferred_element_type=F32,
            )
            total = part if total is None else total + part
        return total

    def send_v(stage, source_of, target_of):
        copies = []
        for step in sorted(range(1, nv), key=lambda step: -min(step, nv - step)):
            peer = (me + step) % nv
            copy = pltpu.make_async_remote_copy(
                src_ref=source_of(peer),
                dst_ref=target_of(me),
                send_sem=v_send.at[stage, step - 1],
                recv_sem=v_recv.at[stage, step - 1],
                device_id={"valve": peer},
                device_id_type=MESH,
            )
            copy.start()
            copies.append(copy)
        return copies

    def exchange(tile, selection, first, last):
        outgoing[tile] = selected(selection, first, last).reshape(nv, 8, POINTS)
        copies = send_v(tile, lambda peer: outgoing.at[tile, peer], lambda mine: arrived.at[tile, mine])
        arrived[tile, me] = outgoing[tile, me]
        return copies

    sent = []
    interpolate((0, 1))
    sent += exchange(0, select_first, 0, 2)
    interpolate((2, 3))
    sent += exchange(1, select_second, 1, 4)
    interpolate((4,))
    sent += exchange(2, select_third, 3, 5)
    extra = selected(select_extra, 4, 5)
    for device in range(nv):
        extra_out[device] = extra[device : device + 1, :]
    sent += send_v(3, lambda peer: extra_out.at[peer], lambda mine: extra_in.at[mine])
    extra_in[me] = extra_out[me]

    arrive(sent)
    for source in range(nv):
        base = source * CAPACITY
        for c in range(5):
            slot = 0
            while slot < CAPACITY:
                number = c * CAPACITY + slot
                if number == 24:
                    fringe_ref[c, base + slot : base + slot + 1, :] = extra_in[source]
                    break
                row = number % 8
                count = min(CAPACITY - slot, 8 - row)
                fringe_ref[c, base + slot : base + slot + count, :] = arrived[number // 8, source, row : row + count, :]
                slot += count

    for copies in (low_y, up_y, low_x, up_x, off_y, off_x, sent):
        for copy in copies:
            copy.wait_send()


def whole(nx, nv, rhs, diag, lower, upper, index, weight, count, owner):
    hbm = pl.BlockSpec(memory_space=pl.ANY)
    vmem = pl.BlockSpec(memory_space=VMEM)
    return pl.pallas_call(
        functools.partial(whole_kernel, nx, nv),
        out_shape=(
            VMEM((5, PLANES, CELLS), F32),
            VMEM((5, nv * CAPACITY, POINTS), F32),
        ),
        in_specs=[hbm] * 8,
        out_specs=(vmem, vmem),
        scratch_shapes=[
            VMEM((5, PLANES, CELLS), F32),
            VMEM((5, 5, PLANES, CELLS), F32),
            VMEM((5, 5, PLANES, CELLS), F32),
            VMEM((5, 5, PLANES, CELLS), F32),
            VMEM((BLOCKS, 8, POINTS), jnp.int32),
            VMEM((BLOCKS, 8, POINTS), F32),
            pltpu.SMEM((1, BLOCKS), jnp.int32),
            pltpu.SMEM((1, BLOCKS), jnp.int32),
            VMEM((ROWS, CELLS), F32),
            VMEM((NY * ROWS, CELLS), F32),
            VMEM((ROWS, CELLS), F32),
            VMEM((nx * ROWS, CELLS), F32),
            VMEM((ROWS, CELLS), F32),
            VMEM((NY * ROWS, CELLS), F32),
            VMEM((ROWS, CELLS), F32),
            VMEM((nx * ROWS, CELLS), F32),
            VMEM((8, CELLS), F32),
            VMEM((NY * 8, CELLS), F32),
            VMEM((8, CELLS), F32),
            VMEM((nx * 8, CELLS), F32),
            VMEM((3, 5, 5, 8, CELLS), F32),
            VMEM((3, 5, 5, 8, CELLS), F32),
            VMEM((5, PLANES, 8, CELLS), F32),
            VMEM((5, BLOCKS * 8, POINTS), F32),
            VMEM((nv * 8, 2 * CELLS), F32),
            VMEM((nv * 8, 3 * CELLS), F32),
            VMEM((nv * 8, 2 * CELLS), F32),
            VMEM((nv, CELLS), F32),
            VMEM((3, nv, 8, POINTS), F32),
            VMEM((3, nv, 8, POINTS), F32),
            VMEM((nv, 1, POINTS), F32),
            VMEM((nv, 1, POINTS), F32),
            pltpu.SemaphoreType.DMA((8,)),
            pltpu.SemaphoreType.DMA((3, NY - 1)),
            pltpu.SemaphoreType.DMA((3, NY - 1)),
            pltpu.SemaphoreType.DMA((3, nx - 1)),
            pltpu.SemaphoreType.DMA((3, nx - 1)),
            pltpu.SemaphoreType.DMA((4, nv - 1)),
            pltpu.SemaphoreType.DMA((4, nv - 1)),
        ],
        compiler_params=pltpu.CompilerParams(collective_id=0, has_side_effects=True),
    )(rhs, diag, lower, upper, index, weight, count, owner)


def solution(mesh):
    nx = mesh.shape["bulk"] // NY
    nv = mesh.shape["valve"]

    def body(rhs, diag, lower, upper, index, weight, count, owner):
        update, rows = whole(nx, nv, rhs, diag, lower, upper, index[0], weight[0], count, owner)
        return update, jnp.transpose(rows, (1, 0, 2))[None]

    in_specs = (
        P(None, "bulk", "valve"),
        P(None, None, "bulk", "valve"),
        P(None, None, "bulk", "valve"),
        P(None, None, "bulk", "valve"),
        P("bulk", "valve", None, None),
        P("bulk", "valve", None, None),
        P("bulk", "valve"),
        P("bulk", "valve"),
    )
    out_specs = (P(None, "bulk", "valve"), P("bulk", "valve", None, None))
    return jax.shard_map(body, mesh=mesh, in_specs=in_specs, out_specs=out_specs, check_vma=False)
```

```python
import functools

import jax
import jax.numpy as jnp
from jax import lax
from jax.experimental import pallas as pl
from jax.experimental.pallas import tpu as pltpu
from jax.sharding import PartitionSpec as P

NY = 8
PLANES = 8
CELLS = 128
POINTS = 128
CAPACITY = 5
ROWS = 32
BLOCKS = 16
MESH = pl.DeviceIdType.MESH
VMEM = pltpu.VMEM
F32 = jnp.float32


def compose(left, right):
    total = left[:, 0][:, None] * right[0][None]
    for c in range(1, 5):
        total = total + left[:, c][:, None] * right[c][None]
    return total


def apply(matrices, vectors):
    total = matrices[:, 0] * vectors[0][None]
    for c in range(1, 5):
        total = total + matrices[:, c] * vectors[c][None]
    return total


def shifted(value, amount):
    shape = value.shape
    flat = value.reshape((-1,) + shape[-2:])
    return pltpu.roll(flat, amount % shape[-2], 1).reshape(shape)


def forward_scan(matrices, offsets):
    row = lax.broadcasted_iota(jnp.int32, (8, CELLS), 0)
    for step in (1, 2, 4):
        live = row >= step
        new_offsets = offsets + apply(matrices, shifted(offsets, step))
        new_matrices = compose(matrices, shifted(matrices, step))
        offsets = jnp.where(live[None], new_offsets, offsets)
        matrices = jnp.where(live[None, None], new_matrices, matrices)
    return matrices, offsets


def backward_matrices(matrices, levels_ref):
    row = lax.broadcasted_iota(jnp.int32, (8, CELLS), 0)
    for level, step in enumerate((1, 2, 4)):
        live = row < 8 - step
        levels_ref[level] = jnp.where(live[None, None], matrices, 0.0)
        matrices = jnp.where(live[None, None], compose(matrices, shifted(matrices, -step)), matrices)
    return matrices


def backward_offsets(levels_ref, offsets):
    for level, step in enumerate((1, 2, 4)):
        offsets = offsets + apply(levels_ref[level], shifted(offsets, -step))
    return offsets


def picked_row(values, index):
    row = lax.broadcasted_iota(jnp.int32, (8, CELLS), 0)
    kept = jnp.where((row == index)[None], values, 0.0)
    for step in (1, 2, 4):
        kept = kept + shifted(kept, step)
    return kept


def whole_kernel(
    nx,
    nv,
    rhs_hbm,
    diag_hbm,
    lower_hbm,
    upper_hbm,
    index_hbm,
    weight_hbm,
    count_hbm,
    owner_hbm,
    update_ref,
    fringe_ref,
    rhs_ref,
    diag_ref,
    lower_ref,
    upper_ref,
    index_ref,
    weight_ref,
    count_ref,
    owner_ref,
    low_out,
    low_all,
    low_total,
    low_rows,
    up_out,
    up_all,
    up_total,
    up_rows,
    off_out,
    off_all,
    off_total,
    off_rows,
    plane_levels,
    row_levels,
    table,
    products,
    select_first,
    select_second,
    select_third,
    select_extra,
    outgoing,
    arrived,
    extra_out,
    extra_in,
    load_sem,
    y_send,
    y_recv,
    x_send,
    x_recv,
    v_send,
    v_recv,
):
    loads = []
    for number, (source, target) in enumerate(
        (
            (diag_hbm, diag_ref),
            (lower_hbm, lower_ref),
            (rhs_hbm, rhs_ref),
            (upper_hbm, upper_ref),
            (owner_hbm, owner_ref),
            (count_hbm, count_ref),
            (weight_hbm, weight_ref),
            (index_hbm, index_ref),
        )
    ):
        load = pltpu.make_async_copy(source, target, load_sem.at[number])
        load.start()
        loads.append(load)
    me = lax.axis_index("valve")
    blocks = BLOCKS
    bulk = lax.axis_index("bulk")
    my_x = bulk // NY
    my_y = bulk % NY

    def y_peer(step):
        return {"bulk": my_x * NY + (my_y + step) % NY}

    def x_peer(step):
        return {"bulk": ((my_x + step) % nx) * NY + my_y}

    barrier = pltpu.get_barrier_semaphore()
    for step in sorted(range(1, nv), key=lambda step: -min(step, nv - step)):
        pl.semaphore_signal(barrier, inc=1, device_id={"valve": (me + step) % nv}, device_id_type=MESH)
        if step < NY:
            near = (4, 3, 5, 2, 6, 1, 7)[NY - 1 - step]
            pl.semaphore_signal(barrier, inc=1, device_id=y_peer(near), device_id_type=MESH)
    for step in range(1, nx):
        pl.semaphore_signal(barrier, inc=1, device_id=x_peer(step), device_id_type=MESH)

    def place(ref, index, rows):
        return ref.at[pl.ds(pl.multiple_of(index * rows, 8), rows), :]

    def send_y(stage, source, target, rows):
        copies = []
        for step in (4, 3, 5, 2, 6, 1, 7):
            copy = pltpu.make_async_remote_copy(
                src_ref=source,
                dst_ref=place(target, my_y, rows),
                send_sem=y_send.at[stage, step - 1],
                recv_sem=y_recv.at[stage, step - 1],
                device_id=y_peer(step),
                device_id_type=MESH,
            )
            copy.start()
            copies.append(copy)
        return copies

    def send_x(stage, source, target, rows):
        copies = []
        for step in range(1, nx):
            copy = pltpu.make_async_remote_copy(
                src_ref=source,
                dst_ref=place(target, my_x, rows),
                send_sem=x_send.at[stage, step - 1],
                recv_sem=x_recv.at[stage, step - 1],
                device_id=x_peer(step),
                device_id_type=MESH,
            )
            copy.start()
            copies.append(copy)
        return copies

    def arrive(copies):
        for copy in copies:
            copy.wait_recv()

    def put(ref, first, value, row):
        for index in range(value.shape[0]):
            ref[first + index : first + index + 1, :] = value[index, row : row + 1, :]

    def gathered(ref, first, count, stride):
        return jnp.stack([ref[pl.ds(first + index, 8, stride=stride), :] for index in range(count)])

    for load in loads[:3]:
        load.wait()
    diag = diag_ref[...]
    low_matrices, low_offsets = forward_scan(-compose(diag, lower_ref[...]), apply(diag, rhs_ref[...]))
    put(low_out, 0, low_matrices.reshape(25, PLANES, CELLS), PLANES - 1)
    put(low_out, 25, low_offsets, PLANES - 1)
    place(low_all, my_y, ROWS)[...] = low_out[...]
    pl.semaphore_wait(barrier, NY + nx + nv - 3)
    low_y = send_y(0, low_out, low_all, ROWS)

    loads[3].wait()
    up_matrices = backward_matrices(-compose(diag, upper_ref[...]), plane_levels)
    put(up_out, 0, up_matrices.reshape(25, PLANES, CELLS), 0)
    place(up_all, my_y, ROWS)[...] = up_out[...]

    for load in loads[4:]:
        load.wait()
    lane = lax.broadcasted_iota(jnp.int32, (1, CELLS), 1)
    block_of = lane >> 3
    owner = jnp.zeros((1, CELLS), jnp.int32)
    for block in range(blocks):
        owner = jnp.where(block_of == block, owner_ref[0, block], owner)
    rank = jnp.zeros((1, CELLS), jnp.int32)
    for earlier in range(blocks):
        same = (owner == owner_ref[0, earlier]) & (block_of > earlier)
        rank = rank + jnp.where(same, 1, 0)
    goal = owner * CAPACITY + rank
    line = lax.broadcasted_iota(jnp.int32, (nv * 8, CELLS), 0)
    for tile, (selection, first, last) in enumerate(
        ((select_first, 0, 2), (select_second, 1, 4), (select_third, 3, 5))
    ):
        number = tile * 8 + (line & 7)
        component = (number * 13) >> 6
        wanted = (line >> 3) * CAPACITY + number - component * CAPACITY
        for c in range(first, last):
            hit = (component == c) & (wanted == goal)
            selection[:, (c - first) * CELLS : (c - first + 1) * CELLS] = jnp.where(hit, 1.0, 0.0).astype(F32)
    wanted = lax.broadcasted_iota(jnp.int32, (nv, CELLS), 0) * CAPACITY + CAPACITY - 1
    select_extra[...] = jnp.where(wanted == goal, 1.0, 0.0).astype(F32)
    for block in range(blocks):
        weight_ref[block] = jnp.where(lane < count_ref[0, block], weight_ref[block], 0.0)

    for copy in low_y:
        copy.wait_send()
    up_y = send_y(1, up_out, up_all, ROWS)
    arrive(low_y)
    row_matrices, row_offsets = forward_scan(
        gathered(low_all, 0, 25, ROWS).reshape(5, 5, 8, CELLS), gathered(low_all, 25, 5, ROWS)
    )
    put(low_total, 0, row_matrices.reshape(25, 8, CELLS), 7)
    put(low_total, 25, row_offsets, 7)
    low_x = send_x(0, low_total, low_rows, ROWS)

    place(low_rows, my_x, ROWS)[...] = low_total[...]

    def chain(rows, offsets_of, order, passes):
        state = [jnp.zeros((1, CELLS), F32) for _ in range(5)]
        for x in order:
            offsets = offsets_of(x)
            new_state = []
            for a in range(5):
                value = offsets[a]
                for b in range(5):
                    at = x * ROWS + a * 5 + b
                    value = value + rows[at : at + 1, :] * state[b]
                new_state.append(value)
            keep = passes(x)
            state = [jnp.where(keep, new, old) for new, old in zip(new_state, state)]
        return jnp.stack([jnp.broadcast_to(value, (8, CELLS)) for value in state])

    arrive(low_x)
    entering = chain(
        low_rows,
        lambda x: [low_rows[x * ROWS + 25 + a : x * ROWS + 26 + a, :] for a in range(5)],
        range(nx - 1),
        lambda x: x < my_x,
    )
    leaving = row_offsets + apply(row_matrices, entering)
    incoming = jnp.where(my_y == 0, entering, picked_row(leaving, my_y - 1))
    starred = low_offsets + apply(low_matrices, incoming)

    partial = backward_offsets(plane_levels, starred)
    put(off_out, 0, partial, 0)
    off_y = send_y(2, off_out, off_all, 8)
    place(off_all, my_y, 8)[...] = off_out[...]

    arrive(up_y)
    row_up = backward_matrices(gathered(up_all, 0, 25, ROWS).reshape(5, 5, 8, CELLS), row_levels)
    put(up_total, 0, row_up.reshape(25, 8, CELLS), 0)
    up_x = send_x(1, up_total, up_rows, ROWS)
    place(up_rows, my_x, ROWS)[...] = up_total[...]

    arrive(off_y)
    row_partial = backward_offsets(row_levels, gathered(off_all, 0, 5, 8))
    put(off_total, 0, row_partial, 0)
    off_x = send_x(2, off_total, off_rows, 8)
    place(off_rows, my_x, 8)[...] = off_total[...]
    arrive(up_x)
    arrive(off_x)
    entering = chain(
        up_rows,
        lambda x: [off_rows[x * 8 + a : x * 8 + a + 1, :] for a in range(5)],
        range(nx - 1, 0, -1),
        lambda x: x > my_x,
    )
    leaving = row_partial + apply(row_up, entering)
    incoming = jnp.where(my_y == NY - 1, entering, picked_row(leaving, my_y + 1))
    update = partial + apply(up_matrices, incoming)
    update_ref[...] = update
    for c in range(5):
        for plane in range(PLANES):
            table[c, plane] = jnp.broadcast_to(update[c, plane : plane + 1, :], (8, CELLS))

    def interpolate(components):
        def step(block, carry):
            donors = index_ref[block]
            weights = weight_ref[block]
            cell = donors & (CELLS - 1)
            plane_of = donors >> 7
            here = [plane_of == plane for plane in range(PLANES)]
            for c in components:
                picked = jnp.take_along_axis(table[c, 0], cell, axis=1, mode="promise_in_bounds")
                for plane in range(1, PLANES):
                    other = jnp.take_along_axis(table[c, plane], cell, axis=1, mode="promise_in_bounds")
                    picked = jnp.where(here[plane], other, picked)
                products[c, pl.ds(pl.multiple_of(block * 8, 8), 8), :] = weights * picked
            return carry

        lax.fori_loop(0, blocks, step, 0, unroll=2)

    def selected(selection, first, last):
        total = None
        for c in range(first, last):
            part = jnp.dot(
                selection[:, (c - first) * CELLS : (c - first + 1) * CELLS],
                products[c],
                precision=lax.Precision.HIGHEST,
                preferred_element_type=F32,
            )
            total = part if total is None else total + part
        return total

    def send_v(stage, source_of, target_of):
        copies = []
        for step in sorted(range(1, nv), key=lambda step: -min(step, nv - step)):
            peer = (me + step) % nv
            copy = pltpu.make_async_remote_copy(
                src_ref=source_of(peer),
                dst_ref=target_of(me),
                send_sem=v_send.at[stage, step - 1],
                recv_sem=v_recv.at[stage, step - 1],
                device_id={"valve": peer},
                device_id_type=MESH,
            )
            copy.start()
            copies.append(copy)
        return copies

    def exchange(tile, selection, first, last):
        outgoing[tile] = selected(selection, first, last).reshape(nv, 8, POINTS)
        copies = send_v(tile, lambda peer: outgoing.at[tile, peer], lambda mine: arrived.at[tile, mine])
        arrived[tile, me] = outgoing[tile, me]
        return copies

    sent = []
    interpolate((0, 1))
    sent += exchange(0, select_first, 0, 2)
    interpolate((2, 3))
    sent += exchange(1, select_second, 1, 4)
    interpolate((4,))
    sent += exchange(2, select_third, 3, 5)
    extra = selected(select_extra, 4, 5)
    for device in range(nv):
        extra_out[device] = extra[device : device + 1, :]
    sent += send_v(3, lambda peer: extra_out.at[peer], lambda mine: extra_in.at[mine])
    extra_in[me] = extra_out[me]

    arrive(sent)
    for source in range(nv):
        base = source * CAPACITY
        for c in range(5):
            slot = 0
            while slot < CAPACITY:
                number = c * CAPACITY + slot
                if number == 24:
                    fringe_ref[c, base + slot : base + slot + 1, :] = extra_in[source]
                    break
                row = number % 8
                count = min(CAPACITY - slot, 8 - row)
                fringe_ref[c, base + slot : base + slot + count, :] = arrived[number // 8, source, row : row + count, :]
                slot += count

    for copies in (up_y, low_x, up_x, off_y, off_x, sent):
        for copy in copies:
            copy.wait_send()


def whole(nx, nv, rhs, diag, lower, upper, index, weight, count, owner):
    hbm = pl.BlockSpec(memory_space=pl.ANY)
    vmem = pl.BlockSpec(memory_space=VMEM)
    return pl.pallas_call(
        functools.partial(whole_kernel, nx, nv),
        out_shape=(
            VMEM((5, PLANES, CELLS), F32),
            VMEM((5, nv * CAPACITY, POINTS), F32),
        ),
        in_specs=[hbm] * 8,
        out_specs=(vmem, vmem),
        scratch_shapes=[
            VMEM((5, PLANES, CELLS), F32),
            VMEM((5, 5, PLANES, CELLS), F32),
            VMEM((5, 5, PLANES, CELLS), F32),
            VMEM((5, 5, PLANES, CELLS), F32),
            VMEM((BLOCKS, 8, POINTS), jnp.int32),
            VMEM((BLOCKS, 8, POINTS), F32),
            pltpu.SMEM((1, BLOCKS), jnp.int32),
            pltpu.SMEM((1, BLOCKS), jnp.int32),
            VMEM((ROWS, CELLS), F32),
            VMEM((NY * ROWS, CELLS), F32),
            VMEM((ROWS, CELLS), F32),
            VMEM((nx * ROWS, CELLS), F32),
            VMEM((ROWS, CELLS), F32),
            VMEM((NY * ROWS, CELLS), F32),
            VMEM((ROWS, CELLS), F32),
            VMEM((nx * ROWS, CELLS), F32),
            VMEM((8, CELLS), F32),
            VMEM((NY * 8, CELLS), F32),
            VMEM((8, CELLS), F32),
            VMEM((nx * 8, CELLS), F32),
            VMEM((3, 5, 5, 8, CELLS), F32),
            VMEM((3, 5, 5, 8, CELLS), F32),
            VMEM((5, PLANES, 8, CELLS), F32),
            VMEM((5, BLOCKS * 8, POINTS), F32),
            VMEM((nv * 8, 2 * CELLS), F32),
            VMEM((nv * 8, 3 * CELLS), F32),
            VMEM((nv * 8, 2 * CELLS), F32),
            VMEM((nv, CELLS), F32),
            VMEM((3, nv, 8, POINTS), F32),
            VMEM((3, nv, 8, POINTS), F32),
            VMEM((nv, 1, POINTS), F32),
            VMEM((nv, 1, POINTS), F32),
            pltpu.SemaphoreType.DMA((8,)),
            pltpu.SemaphoreType.DMA((3, NY - 1)),
            pltpu.SemaphoreType.DMA((3, NY - 1)),
            pltpu.SemaphoreType.DMA((3, nx - 1)),
            pltpu.SemaphoreType.DMA((3, nx - 1)),
            pltpu.SemaphoreType.DMA((4, nv - 1)),
            pltpu.SemaphoreType.DMA((4, nv - 1)),
        ],
        compiler_params=pltpu.CompilerParams(collective_id=0, has_side_effects=True),
    )(rhs, diag, lower, upper, index, weight, count, owner)


def solution(mesh):
    nx = mesh.shape["bulk"] // NY
    nv = mesh.shape["valve"]

    def body(rhs, diag, lower, upper, index, weight, count, owner):
        update, rows = whole(nx, nv, rhs, diag, lower, upper, index[0], weight[0], count, owner)
        return update, jnp.transpose(rows, (1, 0, 2))[None]

    in_specs = (
        P(None, "bulk", "valve"),
        P(None, None, "bulk", "valve"),
        P(None, None, "bulk", "valve"),
        P(None, None, "bulk", "valve"),
        P("bulk", "valve", None, None),
        P("bulk", "valve", None, None),
        P("bulk", "valve"),
        P("bulk", "valve"),
    )
    out_specs = (P(None, "bulk", "valve"), P("bulk", "valve", None, None))
    return jax.shard_map(body, mesh=mesh, in_specs=in_specs, out_specs=out_specs, check_vma=False)
```

```python
import functools

import jax
import jax.numpy as jnp
from jax import lax
from jax.experimental import pallas as pl
from jax.experimental.pallas import tpu as pltpu
from jax.sharding import PartitionSpec as P

NY = 8
PLANES = 8
CELLS = 128
POINTS = 128
CAPACITY = 5
ROWS = 32
BLOCKS = 16
MESH = pl.DeviceIdType.MESH
VMEM = pltpu.VMEM
F32 = jnp.float32


def compose(left, right):
    total = left[:, 0][:, None] * right[0][None]
    for c in range(1, 5):
        total = total + left[:, c][:, None] * right[c][None]
    return total


def apply(matrices, vectors):
    total = matrices[:, 0] * vectors[0][None]
    for c in range(1, 5):
        total = total + matrices[:, c] * vectors[c][None]
    return total


def shifted(value, amount):
    shape = value.shape
    flat = value.reshape((-1,) + shape[-2:])
    return pltpu.roll(flat, amount % shape[-2], 1).reshape(shape)


def forward_scan(matrices, offsets):
    row = lax.broadcasted_iota(jnp.int32, (8, CELLS), 0)
    for step in (1, 2, 4):
        live = row >= step
        new_offsets = offsets + apply(matrices, shifted(offsets, step))
        new_matrices = compose(matrices, shifted(matrices, step))
        offsets = jnp.where(live[None], new_offsets, offsets)
        matrices = jnp.where(live[None, None], new_matrices, matrices)
    return matrices, offsets


def backward_matrices(matrices, levels_ref):
    row = lax.broadcasted_iota(jnp.int32, (8, CELLS), 0)
    for level, step in enumerate((1, 2, 4)):
        live = row < 8 - step
        levels_ref[level] = jnp.where(live[None, None], matrices, 0.0)
        matrices = jnp.where(live[None, None], compose(matrices, shifted(matrices, -step)), matrices)
    return matrices


def backward_offsets(levels_ref, offsets):
    for level, step in enumerate((1, 2, 4)):
        offsets = offsets + apply(levels_ref[level], shifted(offsets, -step))
    return offsets


def picked_row(values, index):
    row = lax.broadcasted_iota(jnp.int32, (8, CELLS), 0)
    kept = jnp.where((row == index)[None], values, 0.0)
    for step in (1, 2, 4):
        kept = kept + shifted(kept, step)
    return kept


def whole_kernel(
    nx,
    nv,
    rhs_hbm,
    diag_hbm,
    lower_hbm,
    upper_hbm,
    index_hbm,
    weight_hbm,
    count_hbm,
    owner_hbm,
    update_ref,
    fringe_ref,
    rhs_ref,
    diag_ref,
    lower_ref,
    upper_ref,
    index_ref,
    weight_ref,
    count_ref,
    owner_ref,
    low_out,
    low_all,
    low_total,
    low_rows,
    up_out,
    up_all,
    up_total,
    up_rows,
    off_out,
    off_all,
    off_total,
    off_rows,
    plane_levels,
    row_levels,
    table,
    products,
    select_first,
    select_second,
    select_third,
    select_extra,
    outgoing,
    arrived,
    extra_out,
    extra_in,
    load_sem,
    y_send,
    y_recv,
    x_send,
    x_recv,
    v_send,
    v_recv,
):
    loads = []
    for number, (source, target) in enumerate(
        (
            (diag_hbm, diag_ref),
            (lower_hbm, lower_ref),
            (rhs_hbm, rhs_ref),
            (upper_hbm, upper_ref),
            (owner_hbm, owner_ref),
            (count_hbm, count_ref),
            (weight_hbm, weight_ref),
            (index_hbm, index_ref),
        )
    ):
        load = pltpu.make_async_copy(source, target, load_sem.at[number])
        load.start()
        loads.append(load)
    me = lax.axis_index("valve")
    blocks = BLOCKS
    bulk = lax.axis_index("bulk")
    my_x = bulk // NY
    my_y = bulk % NY

    def y_peer(step):
        return {"bulk": my_x * NY + (my_y + step) % NY}

    def x_peer(step):
        return {"bulk": ((my_x + step) % nx) * NY + my_y}

    barrier = pltpu.get_barrier_semaphore()
    for step in sorted(range(1, nv), key=lambda step: -min(step, nv - step)):
        pl.semaphore_signal(barrier, inc=1, device_id={"valve": (me + step) % nv}, device_id_type=MESH)
        if step < NY:
            near = (4, 3, 5, 2, 6, 1, 7)[NY - 1 - step]
            pl.semaphore_signal(barrier, inc=1, device_id=y_peer(near), device_id_type=MESH)
    for step in range(1, nx):
        pl.semaphore_signal(barrier, inc=1, device_id=x_peer(step), device_id_type=MESH)

    def place(ref, index, rows):
        return ref.at[pl.ds(pl.multiple_of(index * rows, 8), rows), :]

    def send_y(stage, source, target, rows):
        copies = []
        for step in (4, 3, 5, 2, 6, 1, 7):
            copy = pltpu.make_async_remote_copy(
                src_ref=source,
                dst_ref=place(target, my_y, rows),
                send_sem=y_send.at[stage, step - 1],
                recv_sem=y_recv.at[stage, step - 1],
                device_id=y_peer(step),
                device_id_type=MESH,
            )
            copy.start()
            copies.append(copy)
        return copies

    def send_x(stage, source, target, rows):
        copies = []
        for step in range(1, nx):
            copy = pltpu.make_async_remote_copy(
                src_ref=source,
                dst_ref=place(target, my_x, rows),
                send_sem=x_send.at[stage, step - 1],
                recv_sem=x_recv.at[stage, step - 1],
                device_id=x_peer(step),
                device_id_type=MESH,
            )
            copy.start()
            copies.append(copy)
        return copies

    def arrive(copies):
        for copy in copies:
            copy.wait_recv()

    def put(ref, first, value, row):
        for index in range(value.shape[0]):
            ref[first + index : first + index + 1, :] = value[index, row : row + 1, :]

    def gathered(ref, first, count, stride):
        return jnp.stack([ref[pl.ds(first + index, 8, stride=stride), :] for index in range(count)])

    for load in loads[:3]:
        load.wait()
    diag = diag_ref[...]
    low_matrices, low_offsets = forward_scan(-compose(diag, lower_ref[...]), apply(diag, rhs_ref[...]))
    put(low_out, 0, low_matrices.reshape(25, PLANES, CELLS), PLANES - 1)
    put(low_out, 25, low_offsets, PLANES - 1)
    place(low_all, my_y, ROWS)[...] = low_out[...]
    pl.semaphore_wait(barrier, NY + nx + nv - 3)
    low_y = send_y(0, low_out, low_all, ROWS)

    loads[3].wait()
    up_matrices = backward_matrices(-compose(diag, upper_ref[...]), plane_levels)
    put(up_out, 0, up_matrices.reshape(25, PLANES, CELLS), 0)
    place(up_all, my_y, ROWS)[...] = up_out[...]

    for load in loads[4:]:
        load.wait()
    lane = lax.broadcasted_iota(jnp.int32, (1, CELLS), 1)
    block_of = lane >> 3
    owner = jnp.zeros((1, CELLS), jnp.int32)
    for block in range(blocks):
        owner = jnp.where(block_of == block, owner_ref[0, block], owner)
    rank = jnp.zeros((1, CELLS), jnp.int32)
    for earlier in range(blocks):
        same = (owner == owner_ref[0, earlier]) & (block_of > earlier)
        rank = rank + jnp.where(same, 1, 0)
    goal = owner * CAPACITY + rank
    line = lax.broadcasted_iota(jnp.int32, (nv * 8, CELLS), 0)
    for tile, (selection, first, last) in enumerate(
        ((select_first, 0, 2), (select_second, 1, 4), (select_third, 3, 5))
    ):
        number = tile * 8 + (line & 7)
        component = (number * 13) >> 6
        wanted = (line >> 3) * CAPACITY + number - component * CAPACITY
        for c in range(first, last):
            hit = (component == c) & (wanted == goal)
            selection[:, (c - first) * CELLS : (c - first + 1) * CELLS] = jnp.where(hit, 1.0, 0.0).astype(F32)
    wanted = lax.broadcasted_iota(jnp.int32, (nv, CELLS), 0) * CAPACITY + CAPACITY - 1
    select_extra[...] = jnp.where(wanted == goal, 1.0, 0.0).astype(F32)
    for block in range(blocks):
        weight_ref[block] = jnp.where(lane < count_ref[0, block], weight_ref[block], 0.0)

    for copy in low_y:
        copy.wait_send()
    up_y = send_y(1, up_out, up_all, ROWS)
    arrive(low_y)
    row_matrices, row_offsets = forward_scan(
        gathered(low_all, 0, 25, ROWS).reshape(5, 5, 8, CELLS), gathered(low_all, 25, 5, ROWS)
    )
    put(low_total, 0, row_matrices.reshape(25, 8, CELLS), 7)
    put(low_total, 25, row_offsets, 7)
    low_x = send_x(0, low_total, low_rows, ROWS)

    place(low_rows, my_x, ROWS)[...] = low_total[...]

    def chain(rows, offsets_of, order, passes):
        state = [jnp.zeros((1, CELLS), F32) for _ in range(5)]
        for x in order:
            offsets = offsets_of(x)
            new_state = []
            for a in range(5):
                value = offsets[a]
                for b in range(5):
                    at = x * ROWS + a * 5 + b
                    value = value + rows[at : at + 1, :] * state[b]
                new_state.append(value)
            keep = passes(x)
            state = [jnp.where(keep, new, old) for new, old in zip(new_state, state)]
        return jnp.stack([jnp.broadcast_to(value, (8, CELLS)) for value in state])

    arrive(low_x)
    entering = chain(
        low_rows,
        lambda x: [low_rows[x * ROWS + 25 + a : x * ROWS + 26 + a, :] for a in range(5)],
        range(nx - 1),
        lambda x: x < my_x,
    )
    leaving = row_offsets + apply(row_matrices, entering)
    incoming = jnp.where(my_y == 0, entering, picked_row(leaving, my_y - 1))
    starred = low_offsets + apply(low_matrices, incoming)

    partial = backward_offsets(plane_levels, starred)
    put(off_out, 0, partial, 0)
    off_y = send_y(2, off_out, off_all, 8)
    place(off_all, my_y, 8)[...] = off_out[...]

    arrive(up_y)
    row_up = backward_matrices(gathered(up_all, 0, 25, ROWS).reshape(5, 5, 8, CELLS), row_levels)
    put(up_total, 0, row_up.reshape(25, 8, CELLS), 0)
    up_x = send_x(1, up_total, up_rows, ROWS)
    place(up_rows, my_x, ROWS)[...] = up_total[...]

    arrive(off_y)
    row_partial = backward_offsets(row_levels, gathered(off_all, 0, 5, 8))
    put(off_total, 0, row_partial, 0)
    off_x = send_x(2, off_total, off_rows, 8)
    place(off_rows, my_x, 8)[...] = off_total[...]
    arrive(up_x)
    arrive(off_x)
    entering = chain(
        up_rows,
        lambda x: [off_rows[x * 8 + a : x * 8 + a + 1, :] for a in range(5)],
        range(nx - 1, 0, -1),
        lambda x: x > my_x,
    )
    leaving = row_partial + apply(row_up, entering)
    incoming = jnp.where(my_y == NY - 1, entering, picked_row(leaving, my_y + 1))
    update = partial + apply(up_matrices, incoming)
    update_ref[...] = update
    for c in range(5):
        for plane in range(PLANES):
            table[c, plane] = jnp.broadcast_to(update[c, plane : plane + 1, :], (8, CELLS))

    def interpolate(components):
        def step(block, carry):
            donors = index_ref[block]
            weights = weight_ref[block]
            cell = donors & (CELLS - 1)
            plane_of = donors >> 7
            here = [plane_of == plane for plane in range(PLANES)]
            for c in components:
                picked = jnp.take_along_axis(table[c, 0], cell, axis=1, mode="promise_in_bounds")
                for plane in range(1, PLANES):
                    other = jnp.take_along_axis(table[c, plane], cell, axis=1, mode="promise_in_bounds")
                    picked = jnp.where(here[plane], other, picked)
                products[c, pl.ds(pl.multiple_of(block * 8, 8), 8), :] = weights * picked
            return carry

        lax.fori_loop(0, blocks, step, 0, unroll=8)

    def selected(selection, first, last):
        total = None
        for c in range(first, last):
            chosen = selection[:, (c - first) * CELLS : (c - first + 1) * CELLS].astype(jnp.bfloat16)
            rest = products[c]
            for _ in range(3):
                piece = rest.astype(jnp.bfloat16)
                rest = rest - piece.astype(F32)
                part = jnp.dot(chosen, piece, preferred_element_type=F32)
                total = part if total is None else total + part
        return total

    def send_v(stage, source_of, target_of):
        copies = []
        for step in sorted(range(1, nv), key=lambda step: -min(step, nv - step)):
            peer = (me + step) % nv
            copy = pltpu.make_async_remote_copy(
                src_ref=source_of(peer),
                dst_ref=target_of(me),
                send_sem=v_send.at[stage, step - 1],
                recv_sem=v_recv.at[stage, step - 1],
                device_id={"valve": peer},
                device_id_type=MESH,
            )
            copy.start()
            copies.append(copy)
        return copies

    def exchange(tile, selection, first, last):
        outgoing[tile] = selected(selection, first, last).reshape(nv, 8, POINTS)
        copies = send_v(tile, lambda peer: outgoing.at[tile, peer], lambda mine: arrived.at[tile, mine])
        arrived[tile, me] = outgoing[tile, me]
        return copies

    sent = []
    interpolate((0, 1))
    sent += exchange(0, select_first, 0, 2)
    interpolate((2, 3))
    sent += exchange(1, select_second, 1, 4)
    interpolate((4,))
    sent += exchange(2, select_third, 3, 5)
    extra = selected(select_extra, 4, 5)
    for device in range(nv):
        extra_out[device] = extra[device : device + 1, :]
    sent += send_v(3, lambda peer: extra_out.at[peer], lambda mine: extra_in.at[mine])
    extra_in[me] = extra_out[me]

    arrive(sent)
    for source in range(nv):
        base = source * CAPACITY
        for c in range(5):
            slot = 0
            while slot < CAPACITY:
                number = c * CAPACITY + slot
                if number == 24:
                    fringe_ref[c, base + slot : base + slot + 1, :] = extra_in[source]
                    break
                row = number % 8
                count = min(CAPACITY - slot, 8 - row)
                fringe_ref[c, base + slot : base + slot + count, :] = arrived[number // 8, source, row : row + count, :]
                slot += count

    for copies in (up_y, low_x, up_x, off_y, off_x, sent):
        for copy in copies:
            copy.wait_send()


def whole(nx, nv, rhs, diag, lower, upper, index, weight, count, owner):
    hbm = pl.BlockSpec(memory_space=pl.ANY)
    vmem = pl.BlockSpec(memory_space=VMEM)
    return pl.pallas_call(
        functools.partial(whole_kernel, nx, nv),
        out_shape=(
            VMEM((5, PLANES, CELLS), F32),
            VMEM((5, nv * CAPACITY, POINTS), F32),
        ),
        in_specs=[hbm] * 8,
        out_specs=(vmem, vmem),
        scratch_shapes=[
            VMEM((5, PLANES, CELLS), F32),
            VMEM((5, 5, PLANES, CELLS), F32),
            VMEM((5, 5, PLANES, CELLS), F32),
            VMEM((5, 5, PLANES, CELLS), F32),
            VMEM((BLOCKS, 8, POINTS), jnp.int32),
            VMEM((BLOCKS, 8, POINTS), F32),
            pltpu.SMEM((1, BLOCKS), jnp.int32),
            pltpu.SMEM((1, BLOCKS), jnp.int32),
            VMEM((ROWS, CELLS), F32),
            VMEM((NY * ROWS, CELLS), F32),
            VMEM((ROWS, CELLS), F32),
            VMEM((nx * ROWS, CELLS), F32),
            VMEM((ROWS, CELLS), F32),
            VMEM((NY * ROWS, CELLS), F32),
            VMEM((ROWS, CELLS), F32),
            VMEM((nx * ROWS, CELLS), F32),
            VMEM((8, CELLS), F32),
            VMEM((NY * 8, CELLS), F32),
            VMEM((8, CELLS), F32),
            VMEM((nx * 8, CELLS), F32),
            VMEM((3, 5, 5, 8, CELLS), F32),
            VMEM((3, 5, 5, 8, CELLS), F32),
            VMEM((5, PLANES, 8, CELLS), F32),
            VMEM((5, BLOCKS * 8, POINTS), F32),
            VMEM((nv * 8, 2 * CELLS), F32),
            VMEM((nv * 8, 3 * CELLS), F32),
            VMEM((nv * 8, 2 * CELLS), F32),
            VMEM((nv, CELLS), F32),
            VMEM((3, nv, 8, POINTS), F32),
            VMEM((3, nv, 8, POINTS), F32),
            VMEM((nv, 1, POINTS), F32),
            VMEM((nv, 1, POINTS), F32),
            pltpu.SemaphoreType.DMA((8,)),
            pltpu.SemaphoreType.DMA((3, NY - 1)),
            pltpu.SemaphoreType.DMA((3, NY - 1)),
            pltpu.SemaphoreType.DMA((3, nx - 1)),
            pltpu.SemaphoreType.DMA((3, nx - 1)),
            pltpu.SemaphoreType.DMA((4, nv - 1)),
            pltpu.SemaphoreType.DMA((4, nv - 1)),
        ],
        compiler_params=pltpu.CompilerParams(collective_id=0, has_side_effects=True),
    )(rhs, diag, lower, upper, index, weight, count, owner)


def solution(mesh):
    nx = mesh.shape["bulk"] // NY
    nv = mesh.shape["valve"]

    def body(rhs, diag, lower, upper, index, weight, count, owner):
        update, rows = whole(nx, nv, rhs, diag, lower, upper, index[0], weight[0], count, owner)
        return update, jnp.transpose(rows, (1, 0, 2))[None]

    in_specs = (
        P(None, "bulk", "valve"),
        P(None, None, "bulk", "valve"),
        P(None, None, "bulk", "valve"),
        P(None, None, "bulk", "valve"),
        P("bulk", "valve", None, None),
        P("bulk", "valve", None, None),
        P("bulk", "valve"),
        P("bulk", "valve"),
    )
    out_specs = (P(None, "bulk", "valve"), P("bulk", "valve", None, None))
    return jax.shard_map(body, mesh=mesh, in_specs=in_specs, out_specs=out_specs, check_vma=False)
```
